256 devices in a mesh: section: 4 (over y), chan: 64 (over x, z, core).
Axes of the slice: x: 4, y: 4, z: 8, core: 2. Of those that a mesh axis runs over, the one named last changes fastest.
Arguments:
- voltages: bfloat16 [2, 1024, 16, 4096], P(None, 'chan', 'section'), may hold values from -6 to 6
- coefficients: float32 [4, 4096], replicated, may hold values from -0.046875 to 0.046875
- tile_order: int32 [64, 36], P('chan'), may hold values from 0 to 35, each once within a row
- steer_table: bfloat16 [256, 2, 512], replicated, may hold values from -0.1875 to 0.1875
- beam_index: int32 [256, 64], P(None, 'chan'), may hold values from 0 to 255
Outputs:
- visibility: float32 [64, 36, 2, 128, 128], P('chan', 'section')
- beam_power: float32 [2, 256, 16, 4096], P(None, None, 'section', 'chan')
The draws below stay inside these ranges and needn't reach their ends.
Inputs may be any that keep to these rules, and one draw needn't show every extreme that they name: Row g of tile_order lists each of the 36 work items of channel column g exactly once.
All inputs are finite; a program needn't handle non-finite values.
Results may differ from the reference program's by a relative error of at most 0.0029.
Values may be sent and summed in bfloat16 or wider, within the bound.
A program may use at most 64 MiB of HBM per device.

```python
import jax
import jax.numpy as jnp
import numpy as np
from jax import lax

STATIONS = 512
INPUTS = 1024
NCH = 4096
TAPS = 4
FRAMES = 16
AVG = 64
OUT_DEV = 1
OUT_CH = 64
COLUMNS = 64
TB = 128
PAIRS = 36
WORK = 36
NBEAM = 256
NW = 256


def plant(drawn, rng, least, largest):
    longest = drawn.shape.index(max(drawn.shape))
    spots = []
    for shift in (0, 1):
        where = [jax.random.randint(jax.random.fold_in(rng, axis), (), 0, length) for axis, length in enumerate(drawn.shape)]
        where[longest] = (where[longest] + shift) % drawn.shape[longest]
        spots.append(tuple(where))
    return drawn.at[spots[0]].set(least).at[spots[1]].set(largest)


def steps_of(stream_key, shape, cuts, smallest, top_value):
    def one(axis_at, blocks):
        steps = jax.random.uniform(jax.random.fold_in(jax.random.fold_in(stream_key, 6), axis_at), (blocks,), jnp.float32, smallest / len(cuts), top_value / len(cuts))
        return jnp.repeat(jnp.exp(steps), shape[axis_at] // blocks).reshape((-1,) + (1,) * (len(shape) - axis_at - 1))

    loudness = one(*cuts[0])
    for cut in cuts[1:]:
        loudness = loudness * one(*cut)
    return loudness


def scatter_about(stream_key, dims, spread, most, cuts=(), kind=jnp.bfloat16):
    drawn = jax.random.normal(stream_key, dims, jnp.float32) * spread
    if len(cuts) > 0:
        drawn = steps_of(stream_key, dims, cuts, -0.22, 0.18) * drawn
    return jnp.clip(drawn, min=-most, max=most).astype(kind)


def setup_inputs(seed: int = 0) -> dict:
    splits = jax.random.split(jax.random.key(seed), 6)
    voltages = scatter_about(splits[0], (2, INPUTS, FRAMES, NCH), 1.0, 6.0, ((1, 64), (2, 4)))
    coefficients = scatter_about(splits[1], (TAPS, NCH), (TAPS * NCH) ** -0.5, 0.046875, (), jnp.float32)
    tile_order = jax.vmap(lambda own: jax.random.permutation(own, WORK))(jax.random.split(splits[2], COLUMNS)).reshape((COLUMNS, WORK)).astype(jnp.int32)
    steer_table = scatter_about(splits[3], (NW, 2, STATIONS), (2 * STATIONS) ** -0.5, 0.1875)
    beam_index = plant(jax.random.randint(splits[4], (NBEAM, OUT_CH), 0, NW), jax.random.fold_in(splits[4], 1), 0, NW - 1).astype(jnp.int32)
    return dict(voltages=voltages, coefficients=coefficients, tile_order=tile_order, steer_table=steer_table, beam_index=beam_index)


def channelize(input_block, coefficients):
    samples = input_block.astype(jnp.float32)
    filtered = jnp.zeros(samples.shape, jnp.float32)
    for tap_index in range(TAPS):
        delayed = jnp.pad(samples, ((0, 0), (0, 0), (tap_index, 0), (0, 0)))[:, :, :FRAMES, :]
        filtered = filtered + coefficients[tap_index] * delayed
    spectrum = jnp.fft.fft(lax.complex(filtered[0], filtered[1]), axis=-1)
    return jnp.stack([jnp.real(spectrum), jnp.imag(spectrum)]).astype(jnp.bfloat16)


def reference(voltages, coefficients, tile_order, steer_table, beam_index):
    tile_count = INPUTS // TB
    input_starts = jnp.arange(tile_count, dtype=jnp.int32) * TB
    pieces = lax.map(lambda first_input: channelize(lax.dynamic_slice_in_dim(voltages, first_input, TB, 1), coefficients), input_starts)
    spectra = jnp.moveaxis(pieces, 0, 1).reshape(2, INPUTS, FRAMES, NCH)

    row_table = np.array([a for a in range(tile_count) for b in range(a + 1)], np.int32)
    col_table = np.array([b for a in range(tile_count) for b in range(a + 1)], np.int32)
    mean_factor = 1.0 / (FRAMES * AVG)

    def gram_matrix(channel):
        channel_block = lax.dynamic_slice_in_dim(spectra, channel * AVG, AVG, 3).reshape(2, INPUTS, FRAMES * AVG)
        stacked = jnp.concatenate([channel_block[0], channel_block[1]], axis=1)
        swapped = jnp.concatenate([channel_block[1], -channel_block[0]], axis=1)
        real_part = jnp.dot(stacked, stacked.T, preferred_element_type=jnp.float32)
        imag_part = jnp.dot(swapped, stacked.T, preferred_element_type=jnp.float32)
        return jnp.stack([real_part, imag_part]).reshape(2, tile_count, TB, tile_count, TB)

    def column(column_index):
        grams = lax.map(gram_matrix, column_index * OUT_DEV + jnp.arange(OUT_DEV, dtype=jnp.int32))
        work_items = tile_order[column_index]
        local_channel = work_items // PAIRS
        pair_number = work_items % PAIRS
        row_tiles = jnp.asarray(row_table)[pair_number]
        col_tiles = jnp.asarray(col_table)[pair_number]
        return grams[local_channel, :, row_tiles, :, col_tiles, :] * mean_factor

    visibility = lax.map(column, jnp.arange(COLUMNS, dtype=jnp.int32))

    def beam_group(channel):
        weights = steer_table[beam_index[:, channel]].astype(jnp.float32)
        channel_block = lax.dynamic_slice_in_dim(spectra, channel * AVG, AVG, 3).astype(jnp.float32).reshape(2, STATIONS, 2, FRAMES, AVG)
        product = jnp.einsum("bps,qslfc->bpqlfc", weights, channel_block)
        real_part = product[:, 0, 0] - product[:, 1, 1]
        imag_part = product[:, 0, 1] + product[:, 1, 0]
        return real_part * real_part + imag_part * imag_part

    powers = lax.map(beam_group, jnp.arange(OUT_CH, dtype=jnp.int32))
    beam_power = jnp.transpose(powers, (2, 1, 3, 0, 4)).reshape(2, NBEAM, FRAMES, NCH)
    return visibility, beam_power
```

```python
import functools

import jax
import jax.numpy as jnp
import ml_dtypes
import numpy as np
from jax import lax
from jax.experimental import pallas as pl
from jax.experimental.pallas import tpu as pltpu
from jax.sharding import PartitionSpec as P

NSEC = 4
NX, NZ, NCORE = 4, 8, 2
NCHAN = NX * NZ * NCORE
XBLOCK = NZ * NCORE
LOCAL = 16
NCH = 4096
TAPS = 4
NA = 32
NL = 128
AVG = 64
TB = 128
ITEMS = 9
NBEAM = 256
STATIONS = 512
INPUTS = 1024
MEAN = 1.0 / 1024.0
NT = (((1,), (1,)), ((), ()))
NN = (((1,), (0,)), ((), ()))
TN = (((0,), (0,)), ((), ()))
MESH = pl.DeviceIdType.MESH


def split_np(table):
    high = table.astype(ml_dtypes.bfloat16)
    low = (table - high.astype(np.float64)).astype(ml_dtypes.bfloat16)
    return high, low


def tables():
    c = np.arange(NA)
    angle = 2.0 * np.pi / NA * ((c[:, None] * c[None, :]) % NA)
    cosine, sine = np.cos(angle), np.sin(angle)
    first = np.block([[cosine, sine], [-sine, cosine]])
    high, low = split_np(first)
    first = np.concatenate([high, low, high], axis=1)
    channel = np.arange(AVG)
    lane = np.arange(NL)
    angle = 2.0 * np.pi / NCH * ((channel[:, None] * lane[None, :]) % NCH)
    twiddle = np.stack([np.cos(angle), np.sin(angle)]).astype(np.float32)
    group = np.arange(NCHAN)
    angle = 2.0 * np.pi / NCHAN * ((group[:, None] * lane[None, :]) % NCHAN)
    cosine, sine = np.cos(angle), np.sin(angle)
    second = np.stack(
        [np.concatenate([cosine, sine], axis=1), np.concatenate([-sine, cosine], axis=1)], axis=1
    ).reshape(2 * NCHAN, 2 * NL)
    high, low = split_np(second)
    second = np.concatenate([high, low, high], axis=1)
    return jnp.asarray(first), jnp.asarray(twiddle), jnp.asarray(second)


def split(value):
    high = value.astype(jnp.bfloat16)
    return high, (value - high.astype(jnp.float32)).astype(jnp.bfloat16)


def channelize_kernel(own_ref, past_ref, coef_ref, first_ref, twid_ref, second_ref, out_ref, rows_ref):
    for pair in range(2):

        @pl.loop(0, LOCAL)
        def _(i):
            columns = []
            for t2 in range(2):
                t = 2 * pair + t2
                parts = []
                for q in range(2):
                    total = None
                    for p in range(TAPS):
                        source = own_ref[q, i, t - p] if t >= p else past_ref[q, i, t - p + TAPS - 1]
                        term = coef_ref[p] * source.astype(jnp.float32)
                        total = term if total is None else total + term
                    parts.append(total)
                columns.append(jnp.concatenate(parts, axis=0))
            samples = jnp.concatenate(columns, axis=1)
            high, low = split(samples)
            stacked = jnp.concatenate([high, high, low], axis=0)
            section_one = lax.dot_general(
                first_ref[...], stacked, NN, preferred_element_type=jnp.float32
            )
            rows = []
            for t2 in range(2):
                real = section_one[:NA, t2 * NL : (t2 + 1) * NL]
                imag = section_one[NA:, t2 * NL : (t2 + 1) * NL]
                real = jnp.concatenate([real, real], axis=0)
                imag = jnp.concatenate([imag, imag], axis=0)
                cosine, sine = twid_ref[0], twid_ref[1]
                rows.append(
                    jnp.concatenate(
                        [real * cosine + imag * sine, imag * cosine - real * sine], axis=1
                    )
                )
            turned = jnp.concatenate(rows, axis=0)
            high, low = split(turned)
            stacked = jnp.concatenate([high, high, low], axis=1)
            section_two = lax.dot_general(
                second_ref[...], stacked, NT, preferred_element_type=jnp.float32
            )
            rows_ref[pl.ds(i, 2 * NCHAN, stride=LOCAL), :] = section_two

        out_ref[pair] = rows_ref[...].astype(jnp.bfloat16).reshape(NCHAN, 2, LOCAL, NL)


def exchange_kernel(send_ref, all_ref, local_sem, out_sem, in_sem, ysend_sem, yin_sem):
    section = lax.axis_index("section")
    chan = lax.axis_index("chan")
    x, z, core = chan // XBLOCK, (chan % XBLOCK) // NCORE, chan % NCORE
    right, left = (section + 1) % NSEC, (section + NSEC - 1) % NSEC

    def peer_of(dx, j):
        dz, dc = j // NCORE, j % NCORE
        return ((x + dx) % NX) * XBLOCK + ((z + dz) % NZ) * NCORE + (core + dc) % NCORE

    barrier = pltpu.get_barrier_semaphore()

    @pl.loop(1, NCHAN)
    def _(k):
        pl.semaphore_signal(
            barrier, inc=1, device_id=(section, (chan + k) % NCHAN), device_id_type=MESH
        )

    for other in (left, right):
        pl.semaphore_signal(barrier, inc=1, device_id=(other, chan), device_id_type=MESH)
    pl.semaphore_wait(barrier, NCHAN + 1)

    def piece(pair, dx, j):
        peer = peer_of(dx, j)
        return pltpu.make_async_remote_copy(
            src_ref=send_ref.at[pair, peer],
            dst_ref=all_ref.at[section, pair, chan],
            send_sem=out_sem.at[pair, dx],
            recv_sem=in_sem.at[pair, dx],
            device_id=(section, peer),
            device_id_type=MESH,
        )

    def block(sec, pair, dx, half=None):
        start = ((x + NX - dx) % NX) * XBLOCK
        if half is None:
            return all_ref.at[sec, pair, pl.ds(start, XBLOCK)]
        return all_ref.at[sec, pair, pl.ds(start + half * (XBLOCK // 2), XBLOCK // 2)]

    def ycopy(sec, pair, dx, half, target, slot):
        return pltpu.make_async_remote_copy(
            src_ref=block(sec, pair, dx, half),
            dst_ref=block(sec, pair, dx, half),
            send_sem=ysend_sem.at[pair, dx, slot],
            recv_sem=yin_sem.at[pair, dx, slot],
            device_id=(target, chan),
            device_id_type=MESH,
        )

    order = [(pair, dx) for pair in (1, 0) for dx in range(NX)]
    for pair in (1, 0):
        pltpu.make_async_copy(
            send_ref.at[pair, chan], all_ref.at[section, pair, chan], in_sem.at[pair, 0]
        ).start()
        for dx in range(NX):

            @pl.loop(1 if dx == 0 else 0, XBLOCK)
            def _(j):
                piece(pair, dx, j).start()

    def relay(pair, dx):
        ycopy(left, pair, dx, None, right, 0).wait_recv()
        ycopy(left, pair, dx, 0, right, 2).start()
        ycopy(right, pair, dx, None, left, 1).wait_recv()
        ycopy(right, pair, dx, 1, left, 3).start()

    for n, (pair, dx) in enumerate(order):
        mine = block(section, pair, dx)
        pltpu.make_async_copy(mine, mine, in_sem.at[pair, dx]).wait()
        ycopy(section, pair, dx, None, right, 0).start()
        ycopy(section, pair, dx, None, left, 1).start()
        if n > 0:
            relay(*order[n - 1])
    relay(*order[-1])
    far = (section + 2) % NSEC
    for pair, dx in order:
        ycopy(far, pair, dx, 0, right, 2).wait_recv()
        ycopy(far, pair, dx, 1, left, 3).wait_recv()
    for pair, dx in order:
        ycopy(section, pair, dx, None, right, 0).wait_send()
        ycopy(section, pair, dx, None, left, 1).wait_send()
        ycopy(left, pair, dx, 0, right, 2).wait_send()
        ycopy(right, pair, dx, 1, left, 3).wait_send()
        count = XBLOCK - 1 if dx == 0 else XBLOCK
        sent = send_ref.at[pair, pl.ds(0, count)]
        pltpu.make_async_copy(sent, sent, out_sem.at[pair, dx]).wait()


def products_kernel(row_ref, col_ref, all_ref, own_ref, table_ref, index_ref, vis_ref, beam_ref, weight_ref):
    def tile(index, sec, pair):
        part = all_ref[sec, pair, pl.ds(index * (TB // LOCAL), TB // LOCAL)]
        return jnp.concatenate(
            [part[:, 0].reshape(TB, NL), part[:, 1].reshape(TB, NL)], axis=0
        )

    @pl.loop(0, ITEMS)
    def _(r):
        a, b = row_ref[r], col_ref[r]
        spans = [(sec, pair) for sec in range(NSEC) for pair in range(2)]
        left = jnp.concatenate([tile(a, *span) for span in spans], axis=1)
        right = jnp.concatenate([tile(b, *span) for span in spans], axis=1)
        gram = lax.dot_general(left, right, NT, preferred_element_type=jnp.float32)
        vis_ref[0, r, 0] = (gram[:TB, :TB] + gram[TB:, TB:]) * MEAN
        vis_ref[0, r, 1] = (gram[TB:, :TB] - gram[:TB, TB:]) * MEAN

    picked = (
        lax.broadcasted_iota(jnp.int32, (NBEAM, NBEAM), 0) == index_ref[...]
    ).astype(jnp.float32).astype(jnp.bfloat16)
    chosen = lax.dot_general(
        picked, table_ref[...], TN, preferred_element_type=jnp.float32
    ).astype(jnp.bfloat16)
    for l in range(2):
        spread = (
            lax.broadcasted_iota(jnp.int32, (STATIONS, INPUTS), 1)
            == 2 * lax.broadcasted_iota(jnp.int32, (STATIONS, INPUTS), 0) + l
        ).astype(jnp.float32).astype(jnp.bfloat16)
        for q in range(2):
            weight_ref[pl.ds(q * NBEAM, NBEAM), :] = lax.dot_general(
                chosen[:, q * STATIONS : (q + 1) * STATIONS], spread, NN,
                preferred_element_type=jnp.float32,
            ).astype(jnp.bfloat16)
        for pair in range(2):
            spectra = jnp.concatenate(
                [own_ref[0, pair, :, q].reshape(INPUTS, NL) for q in range(2)], axis=1
            )
            sums = lax.dot_general(
                weight_ref[...], spectra, NN, preferred_element_type=jnp.float32
            )
            real = sums[:NBEAM, :NL] - sums[NBEAM:, NL:]
            imag = sums[:NBEAM, NL:] + sums[NBEAM:, :NL]
            power = real * real + imag * imag
            for t2 in range(2):
                beam_ref[l, :, 2 * pair + t2, :] = power[:, t2 * AVG : (t2 + 1) * AVG]


def shards(voltages, coefficients, tile_order, steer_table, beam_index):
    section = lax.axis_index("section")
    own = voltages.reshape(2, LOCAL, 4, NA, NL)
    history = lax.ppermute(own[:, :, 1:], "section", [(i, i + 1) for i in range(NSEC - 1)])
    first, twiddle, second = tables()
    vmem = pl.BlockSpec(memory_space=pltpu.VMEM)
    smem = pl.BlockSpec(memory_space=pltpu.SMEM)
    anywhere = pl.BlockSpec(memory_space=pl.ANY)
    pieces = pl.pallas_call(
        channelize_kernel,
        out_shape=jax.ShapeDtypeStruct((2, NCHAN, 2, LOCAL, NL), jnp.bfloat16),
        in_specs=[vmem] * 6,
        out_specs=vmem,
        scratch_shapes=[pltpu.VMEM((2 * NCHAN * LOCAL, NL), jnp.float32)],
        name="channelize",
    )(own, history, coefficients.reshape(TAPS, NA, NL), first, twiddle, second)
    gathered = pl.pallas_call(
        exchange_kernel,
        out_shape=jax.ShapeDtypeStruct((NSEC, 2, NCHAN, 2, LOCAL, NL), jnp.bfloat16),
        in_specs=[anywhere],
        out_specs=anywhere,
        scratch_shapes=[
            pltpu.SemaphoreType.DMA,
            pltpu.SemaphoreType.DMA((2, NX)),
            pltpu.SemaphoreType.DMA((2, NX)),
            pltpu.SemaphoreType.DMA((2, NX, 4)),
            pltpu.SemaphoreType.DMA((2, NX, 4)),
        ],
        compiler_params=pltpu.CompilerParams(collective_id=0, has_side_effects=True),
        name="exchange",
    )(pieces)
    items = lax.dynamic_slice_in_dim(tile_order[0], section * ITEMS, ITEMS)
    starts = np.array([a * (a + 1) // 2 for a in range(8)], np.int32)
    rows = jnp.sum((starts[None, :] <= items[:, None]).astype(jnp.int32), axis=1) - 1
    cols = items - rows * (rows + 1) // 2
    visibility, beam_power = pl.pallas_call(
        products_kernel,
        out_shape=(
            jax.ShapeDtypeStruct((1, ITEMS, 2, TB, TB), jnp.float32),
            jax.ShapeDtypeStruct((2, NBEAM, 4, AVG), jnp.float32),
        ),
        in_specs=[smem, smem, vmem, vmem, vmem, vmem],
        out_specs=(vmem, vmem),
        scratch_shapes=[pltpu.VMEM((2 * NBEAM, INPUTS), jnp.bfloat16)],
        name="products",
    )(
        rows,
        cols,
        gathered,
        lax.dynamic_slice_in_dim(gathered, section, 1, 0),
        steer_table.reshape(NBEAM, 2 * STATIONS),
        beam_index.reshape(1, NBEAM),
    )
    return visibility, beam_power


def solution(mesh):
    placed = (P(None, "chan", "section", None), P(), P("chan", None), P(), P(None, "chan"))
    return jax.shard_map(
        shards,
        mesh=mesh,
        in_specs=placed,
        out_specs=(P("chan", "section", None, None, None), P(None, None, "section", "chan")),
        check_vma=False,
    )
```

```python
import jax
import jax.numpy as jnp
import ml_dtypes
import numpy as np
from jax import lax
from jax.experimental import pallas as pl
from jax.experimental.pallas import tpu as pltpu
from jax.sharding import PartitionSpec as P

NSEC = 4
NX, NZ, NCORE = 4, 8, 2
NCHAN = NX * NZ * NCORE
XBLOCK = NZ * NCORE
LOCAL = 16
NCH = 4096
TAPS = 4
NA = 32
NL = 128
AVG = 64
TB = 128
ITEMS = 9
UNROLL = 4
NBEAM = 256
STATIONS = 512
INPUTS = 1024
MEAN = 1.0 / 1024.0
NT = (((1,), (1,)), ((), ()))
NN = (((1,), (0,)), ((), ()))
TN = (((0,), (0,)), ((), ()))
MESH = pl.DeviceIdType.MESH


def split_np(table):
    high = table.astype(ml_dtypes.bfloat16)
    low = (table - high.astype(np.float64)).astype(ml_dtypes.bfloat16)
    return high, low


def tables():
    c = np.arange(NA)
    angle = 2.0 * np.pi / NA * ((c[:, None] * c[None, :]) % NA)
    cosine, sine = np.cos(angle), np.sin(angle)
    first = np.block([[cosine, sine], [-sine, cosine]])
    high, low = split_np(first)
    first = np.concatenate([high, low, high], axis=1)
    channel = np.arange(AVG)
    lane = np.arange(NL)
    angle = 2.0 * np.pi / NCH * ((channel[:, None] * lane[None, :]) % NCH)
    twiddle = np.stack([np.cos(angle), np.sin(angle)]).astype(np.float32)
    group = np.arange(NCHAN)
    angle = 2.0 * np.pi / NCHAN * ((group[:, None] * lane[None, :]) % NCHAN)
    cosine, sine = np.cos(angle), np.sin(angle)
    second = np.stack(
        [np.concatenate([cosine, sine], axis=1), np.concatenate([-sine, cosine], axis=1)], axis=1
    ).reshape(2 * NCHAN, 2 * NL)
    high, low = split_np(second)
    second = np.concatenate([high, low, high], axis=1)
    return jnp.asarray(first), jnp.asarray(twiddle), jnp.asarray(second)


def split(value):
    high = value.astype(jnp.bfloat16)
    return high, (value - high.astype(jnp.float32)).astype(jnp.bfloat16)


def stage_one(frame, t2, sources, coef_ref, first_ref, twid_ref, turned_ref):
    @pl.loop(0, LOCAL, step=UNROLL)
    def _(start):
        columns = []
        for u in range(UNROLL):
            parts = []
            for q in range(2):
                total = None
                for p in range(TAPS):
                    term = coef_ref[pl.ds(p * NA, NA), :] * sources(q, start + u, frame - p).astype(jnp.float32)
                    total = term if total is None else total + term
                parts.append(total)
            columns.append(jnp.concatenate(parts, axis=0))
        high, low = split(jnp.concatenate(columns, axis=1))
        section_one = lax.dot_general(
            first_ref[...],
            jnp.concatenate([high, high, low], axis=0),
            NN,
            preferred_element_type=jnp.float32,
        )
        cosine, sine = twid_ref[0], twid_ref[1]
        for u in range(UNROLL):
            real = section_one[:NA, u * NL : (u + 1) * NL]
            imag = section_one[NA:, u * NL : (u + 1) * NL]
            real = jnp.concatenate([real, real], axis=0)
            imag = jnp.concatenate([imag, imag], axis=0)
            high, low = split(
                jnp.concatenate([real * cosine + imag * sine, imag * cosine - real * sine], axis=1)
            )
            turned_ref[start + u, t2 * AVG : (t2 + 1) * AVG, :] = jnp.concatenate([high, low], axis=1)


def stage_two(pair, second_ref, turned_ref, rows_ref, send_ref):
    @pl.loop(0, LOCAL, step=UNROLL)
    def _(start):
        turned = turned_ref[pl.ds(start, UNROLL)].reshape(UNROLL * 2 * AVG, 4 * NL)
        high, low = turned[:, : 2 * NL], turned[:, 2 * NL :]
        section_two = lax.dot_general(
            second_ref[...],
            jnp.concatenate([high, high, low], axis=1),
            NT,
            preferred_element_type=jnp.float32,
        )
        for u in range(UNROLL):
            rows_ref[pl.ds(start + u, 2 * NCHAN, stride=LOCAL), :] = section_two[
                :, u * NL : (u + 1) * NL
            ]

    send_ref[pair] = rows_ref[...].astype(jnp.bfloat16).reshape(NCHAN, 2, LOCAL, NL)


def tile(buffer, index):
    part = buffer[pl.ds(index * (TB // LOCAL), TB // LOCAL)]
    return jnp.concatenate([part[:, 0].reshape(TB, NL), part[:, 1].reshape(TB, NL)], axis=0)


def correlator_kernel(
    own_ref, coefs_ref, first_ref, twid_ref, second_ref, order_ref, table_ref, index_ref,
    vis_ref, beam_ref,
    past_ref, coef_ref, turned_ref, rows_ref, send_ref, mine1, left1, right1, far1,
    mine0, left0, right0, far0, acc_ref, weight_ref,
    past_send, past_recv, out_sem, in_sem, ysend_sem, yin_sem,
):
    section = lax.axis_index("section")
    chan = lax.axis_index("chan")
    x, z, core = chan // XBLOCK, (chan % XBLOCK) // NCORE, chan % NCORE
    right, left = (section + 1) % NSEC, (section + NSEC - 1) % NSEC
    mine, lefts, rights, fars = (mine0, mine1), (left0, left1), (right0, right1), (far0, far1)

    barrier = pltpu.get_barrier_semaphore()

    @pl.loop(1, NCHAN)
    def _(k):
        pl.semaphore_signal(
            barrier, inc=1, device_id=(section, (chan + k) % NCHAN), device_id_type=MESH
        )

    for other in (left, right):
        pl.semaphore_signal(barrier, inc=1, device_id=(other, chan), device_id_type=MESH)

    for a in range(NA):
        coef_ref[pl.ds(a, TAPS, stride=NA), :] = coefs_ref[:, a * NL : (a + 1) * NL]

    def sources(q, i, t):
        return own_ref[q, i, t] if t >= 0 else past_ref[t + TAPS - 1, q, i]

    stage_one(3, 1, sources, coef_ref, first_ref, twid_ref, turned_ref)
    pl.semaphore_wait(barrier, NCHAN + 1)

    def halo(t):
        return pltpu.make_async_remote_copy(
            src_ref=own_ref.at[:, :, t + 4],
            dst_ref=past_ref.at[t + TAPS - 1],
            send_sem=past_send.at[t + TAPS - 1],
            recv_sem=past_recv.at[t + TAPS - 1],
            device_id=(right, chan),
            device_id_type=MESH,
        )

    def halo_wait(t):
        halo(t).wait_recv()

        @pl.when(section == 0)
        def _():
            past_ref[t + TAPS - 1] = jnp.zeros(past_ref.shape[1:], jnp.bfloat16)

    for t in (-1, -2, -3):
        halo(t).start()

    def piece(pair, dx, j):
        dz, dc = j // NCORE, j % NCORE
        peer = ((x + dx) % NX) * XBLOCK + ((z + dz) % NZ) * NCORE + (core + dc) % NCORE
        return pltpu.make_async_remote_copy(
            src_ref=send_ref.at[pair, peer],
            dst_ref=mine[pair].at[chan],
            send_sem=out_sem.at[pair, dx],
            recv_sem=in_sem.at[pair, dx],
            device_id=(section, peer),
            device_id_type=MESH,
        )

    def scatter(pair):
        pltpu.make_async_copy(
            send_ref.at[pair, chan], mine[pair].at[chan], in_sem.at[pair, 0]
        ).start()
        for dx in range(NX):

            @pl.loop(1 if dx == 0 else 0, XBLOCK)
            def _(j):
                piece(pair, dx, j).start()

    def ycopy(source, target, dx, half, peer, pair, slot):
        start = ((x + NX - dx) % NX) * XBLOCK
        count = XBLOCK
        if half is not None:
            count = XBLOCK // 2
            start = start + half * count
        return pltpu.make_async_remote_copy(
            src_ref=source[pair].at[pl.ds(start, count)],
            dst_ref=target[pair].at[pl.ds(start, count)],
            send_sem=ysend_sem.at[pair, dx, slot],
            recv_sem=yin_sem.at[pair, dx, slot],
            device_id=(peer, chan),
            device_id_type=MESH,
        )

    def to_right(pair, dx):
        return ycopy(mine, lefts, dx, None, right, pair, 0)

    def to_left(pair, dx):
        return ycopy(mine, rights, dx, None, left, pair, 1)

    def on_right(pair, dx):
        return ycopy(lefts, fars, dx, 0, right, pair, 2)

    def on_left(pair, dx):
        return ycopy(rights, fars, dx, 1, left, pair, 3)

    def forward(pair, dx):
        part = mine[pair].at[pl.ds(((x + NX - dx) % NX) * XBLOCK, XBLOCK)]
        pltpu.make_async_copy(part, part, in_sem.at[pair, dx]).wait()
        to_right(pair, dx).start()
        to_left(pair, dx).start()

    def relay(pair, dx):
        to_right(pair, dx).wait_recv()
        on_right(pair, dx).start()
        to_left(pair, dx).wait_recv()
        on_left(pair, dx).start()

    def far_wait(pair):
        for dx in range(NX):
            on_right(pair, dx).wait_recv()
            on_left(pair, dx).wait_recv()

    def products(buffers, first, last):
        @pl.loop(0, ITEMS)
        def _(r):
            n = order_ref[0, section * ITEMS + r]
            a = 0
            for k in range(1, INPUTS // TB):
                a = a + (n >= k * (k + 1) // 2).astype(jnp.int32)
            b = n - a * (a + 1) // 2
            gram = lax.dot_general(
                jnp.concatenate([tile(buffer, a) for buffer in buffers], axis=1),
                jnp.concatenate([tile(buffer, b) for buffer in buffers], axis=1),
                NT,
                preferred_element_type=jnp.float32,
            )
            if not first:
                gram = gram + acc_ref[r]
            if last:
                vis_ref[0, r, 0] = (gram[:TB, :TB] + gram[TB:, TB:]) * MEAN
                vis_ref[0, r, 1] = (gram[TB:, :TB] - gram[:TB, TB:]) * MEAN
            else:
                acc_ref[r] = gram

    def weights():
        picked = (
            lax.broadcasted_iota(jnp.int32, (NBEAM, NBEAM), 0) == index_ref[...]
        ).astype(jnp.float32).astype(jnp.bfloat16)
        chosen = lax.dot_general(
            picked, table_ref[...], TN, preferred_element_type=jnp.float32
        ).astype(jnp.bfloat16)
        for l in range(2):
            spread = (
                lax.broadcasted_iota(jnp.int32, (STATIONS, INPUTS), 1)
                == 2 * lax.broadcasted_iota(jnp.int32, (STATIONS, INPUTS), 0) + l
            ).astype(jnp.float32).astype(jnp.bfloat16)
            for q in range(2):
                weight_ref[l, pl.ds(q * NBEAM, NBEAM), :] = lax.dot_general(
                    chosen[:, q * STATIONS : (q + 1) * STATIONS], spread, NN,
                    preferred_element_type=jnp.float32,
                ).astype(jnp.bfloat16)

    def beams(pair, l):
        spectra = jnp.concatenate(
            [mine[pair][:, q].reshape(INPUTS, NL) for q in range(2)], axis=1
        )
        sums = lax.dot_general(weight_ref[l], spectra, NN, preferred_element_type=jnp.float32)
        real = sums[:NBEAM, :NL] - sums[NBEAM:, NL:]
        imag = sums[:NBEAM, NL:] + sums[NBEAM:, :NL]
        power = (real * real + imag * imag).T
        for t2 in range(2):
            beam_ref[l, 2 * pair + t2] = power[t2 * AVG : (t2 + 1) * AVG]

    halo_wait(-1)
    stage_one(2, 0, sources, coef_ref, first_ref, twid_ref, turned_ref)
    stage_two(1, second_ref, turned_ref, rows_ref, send_ref)
    scatter(1)
    halo_wait(-2)
    stage_one(1, 1, sources, coef_ref, first_ref, twid_ref, turned_ref)
    forward(1, 0)
    halo_wait(-3)
    stage_one(0, 0, sources, coef_ref, first_ref, twid_ref, turned_ref)
    forward(1, 1)
    relay(1, 0)
    stage_two(0, second_ref, turned_ref, rows_ref, send_ref)
    scatter(0)
    forward(1, 2)
    relay(1, 1)
    forward(1, 3)
    relay(1, 2)
    weights()
    forward(0, 0)
    relay(1, 3)
    beams(1, 0)
    forward(0, 1)
    relay(0, 0)
    beams(1, 1)
    forward(0, 2)
    relay(0, 1)
    products((mine1, left1, right1), True, False)
    forward(0, 3)
    relay(0, 2)
    far_wait(1)
    products((far1, mine0), False, False)
    relay(0, 3)
    products((left0, right0), False, False)
    beams(0, 0)
    beams(0, 1)
    far_wait(0)
    products((far0,), False, True)

    for t in (-1, -2, -3):
        halo(t).wait_send()
    for pair in (1, 0):
        for dx in range(NX):
            for copy in (to_right, to_left, on_right, on_left):
                copy(pair, dx).wait_send()
            sent = send_ref.at[pair, pl.ds(0, XBLOCK - 1 if dx == 0 else XBLOCK)]
            pltpu.make_async_copy(sent, sent, out_sem.at[pair, dx]).wait()


def shards(voltages, coefficients, tile_order, steer_table, beam_index):
    vmem = pl.BlockSpec(memory_space=pltpu.VMEM)
    smem = pl.BlockSpec(memory_space=pltpu.SMEM)
    frames = pltpu.VMEM((NCHAN, 2, LOCAL, NL), jnp.bfloat16)
    visibility, beam_power = pl.pallas_call(
        correlator_kernel,
        out_shape=(
            jax.ShapeDtypeStruct((1, ITEMS, 2, TB, TB), jnp.float32),
            jax.ShapeDtypeStruct((2, 4, AVG, NBEAM), jnp.float32),
        ),
        in_specs=[vmem, vmem, vmem, vmem, vmem, smem, vmem, vmem],
        out_specs=(vmem, vmem),
        scratch_shapes=[
            pltpu.VMEM((TAPS - 1, 2, LOCAL, NA, NL), jnp.bfloat16),
            pltpu.VMEM((TAPS * NA, NL), jnp.float32),
            pltpu.VMEM((LOCAL, 2 * AVG, 4 * NL), jnp.bfloat16),
            pltpu.VMEM((2 * NCHAN * LOCAL, NL), jnp.float32),
            pltpu.VMEM((2, NCHAN, 2, LOCAL, NL), jnp.bfloat16),
        ]
        + [frames] * 8
        + [
            pltpu.VMEM((ITEMS, 2 * TB, 2 * TB), jnp.float32),
            pltpu.VMEM((2, 2 * NBEAM, INPUTS), jnp.bfloat16),
            pltpu.SemaphoreType.DMA((TAPS - 1,)),
            pltpu.SemaphoreType.DMA((TAPS - 1,)),
            pltpu.SemaphoreType.DMA((2, NX)),
            pltpu.SemaphoreType.DMA((2, NX)),
            pltpu.SemaphoreType.DMA((2, NX, 4)),
            pltpu.SemaphoreType.DMA((2, NX, 4)),
        ],
        compiler_params=pltpu.CompilerParams(
            collective_id=0, has_side_effects=True, vmem_limit_bytes=48 * 1024 * 1024
        ),
        name="correlator",
    )(
        voltages.reshape(2, LOCAL, 4, NA, NL),
        coefficients,
        *tables(),
        tile_order,
        steer_table.reshape(NBEAM, 2 * STATIONS),
        beam_index.reshape(1, NBEAM),
    )
    return visibility, jnp.transpose(beam_power, (0, 3, 1, 2))


def solution(mesh):
    placed = (P(None, "chan", "section", None), P(), P("chan", None), P(), P(None, "chan"))
    return jax.shard_map(
        shards,
        mesh=mesh,
        in_specs=placed,
        out_specs=(P("chan", "section", None, None, None), P(None, None, "section", "chan")),
        check_vma=False,
    )
```

```python
import jax
import jax.numpy as jnp
import ml_dtypes
import numpy as np
from jax import lax
from jax.experimental import pallas as pl
from jax.experimental.pallas import tpu as pltpu
from jax.sharding import PartitionSpec as P

NSEC = 4
FRAMES = 4
NX, NZ, NCORE = 4, 8, 2
NCHAN = NX * NZ * NCORE
XBLOCK = NZ * NCORE
LOCAL = 16
NCH = 4096
TAPS = 4
NA = 32
NL = 128
AVG = 64
TB = 128
ITEMS = 9
UNROLL = 4
NBEAM = 256
STATIONS = 512
INPUTS = 1024
MEAN = 1.0 / 1024.0
NT = (((1,), (1,)), ((), ()))
NN = (((1,), (0,)), ((), ()))
TN = (((0,), (0,)), ((), ()))
MESH = pl.DeviceIdType.MESH
BY_RIGHT = ((0, 1), (0, 3))


def split_np(table):
    high = table.astype(ml_dtypes.bfloat16)
    low = (table - high.astype(np.float64)).astype(ml_dtypes.bfloat16)
    return high, low


def tables():
    c = np.arange(NA)
    angle = 2.0 * np.pi / NA * ((c[:, None] * c[None, :]) % NA)
    cosine, sine = np.cos(angle), np.sin(angle)
    first = np.block([[cosine, sine], [-sine, cosine]])
    high, low = split_np(first)
    first = np.concatenate([high, low, high], axis=1)
    channel = np.arange(AVG)
    lane = np.arange(NL)
    angle = 2.0 * np.pi / NCH * ((channel[:, None] * lane[None, :]) % NCH)
    twiddle = np.stack([np.cos(angle), np.sin(angle)]).astype(np.float32)
    group = np.arange(NCHAN)
    angle = 2.0 * np.pi / NCHAN * ((group[:, None] * lane[None, :]) % NCHAN)
    cosine, sine = np.cos(angle), np.sin(angle)
    second = np.concatenate([cosine, sine], axis=1)
    high, low = split_np(second)
    second = np.concatenate([high, low, high], axis=1)
    return jnp.asarray(first), jnp.asarray(twiddle), jnp.asarray(second)


def split(value):
    high = value.astype(jnp.bfloat16)
    return high, (value - high.astype(jnp.float32)).astype(jnp.bfloat16)


def transform(frame, lower, upper, sources, coef_ref, first_ref, twid_ref, second_ref, rows_ref):
    @pl.loop(lower, upper, step=UNROLL)
    def _(start):
        columns = []
        for u in range(UNROLL):
            parts = []
            for q in range(2):
                total = None
                for p in range(TAPS):
                    term = coef_ref[pl.ds(p * NA, NA), :] * sources(q, start + u, frame - p).astype(jnp.float32)
                    total = term if total is None else total + term
                parts.append(total)
            columns.append(jnp.concatenate(parts, axis=0))
        high, low = split(jnp.concatenate(columns, axis=1))
        section_one = lax.dot_general(
            first_ref[...],
            jnp.concatenate([high, high, low], axis=0),
            NN,
            preferred_element_type=jnp.float32,
        )
        cosine, sine = twid_ref[0], twid_ref[1]
        turned = []
        for u in range(UNROLL):
            real = section_one[:NA, u * NL : (u + 1) * NL]
            imag = section_one[NA:, u * NL : (u + 1) * NL]
            real = jnp.concatenate([real, real], axis=0)
            imag = jnp.concatenate([imag, imag], axis=0)
            real, imag = real * cosine + imag * sine, imag * cosine - real * sine
            rows = jnp.concatenate(
                [jnp.concatenate([real, imag], axis=1), jnp.concatenate([imag, -real], axis=1)], axis=0
            )
            high, low = split(rows)
            turned.append(jnp.concatenate([high, high, low], axis=1))
        section_two = lax.dot_general(
            second_ref[...],
            jnp.concatenate(turned, axis=0),
            NT,
            preferred_element_type=jnp.float32,
        )
        for u in range(UNROLL):
            rows_ref[pl.ds(start + u, NCHAN, stride=LOCAL), :] = section_two[
                :, u * NL : (u + 1) * NL
            ]


def tile(buffer, index):
    return buffer[pl.ds(index * (TB // LOCAL), TB // LOCAL)].reshape(TB, NL)


def turned_tile(buffer, index):
    part = tile(buffer, index)
    return jnp.concatenate([part[:, AVG:], -part[:, :AVG]], axis=1)


def multiply(item, buffers, acc_ref, vis_ref, order_ref, offset, first, last):
    n = order_ref[0, offset + item]
    a = 0
    for k in range(1, INPUTS // TB):
        a = a + (n >= k * (k + 1) // 2).astype(jnp.int32)
    b = n - a * (a + 1) // 2
    straight = jnp.concatenate([tile(buffer, a) for buffer in buffers], axis=1)
    turned = jnp.concatenate([turned_tile(buffer, a) for buffer in buffers], axis=1)
    gram = lax.dot_general(
        jnp.concatenate([straight, turned], axis=0),
        jnp.concatenate([tile(buffer, b) for buffer in buffers], axis=1),
        NT,
        preferred_element_type=jnp.float32,
    )
    if not first:
        gram = gram + acc_ref[item]
    if last:
        vis_ref[0, item] = (gram * MEAN).reshape(2, TB, TB)
    else:
        acc_ref[item] = gram


def make_weights(l, table_ref, index_ref, weight_ref):
    picked = (
        lax.broadcasted_iota(jnp.int32, (NBEAM, NBEAM), 0) == index_ref[...]
    ).astype(jnp.float32).astype(jnp.bfloat16)
    chosen = lax.dot_general(
        picked, table_ref[...], TN, preferred_element_type=jnp.float32
    ).astype(jnp.bfloat16)
    spread = (
        lax.broadcasted_iota(jnp.int32, (STATIONS, INPUTS), 1)
        == 2 * lax.broadcasted_iota(jnp.int32, (STATIONS, INPUTS), 0) + l
    ).astype(jnp.float32).astype(jnp.bfloat16)
    for q in range(2):
        weight_ref[l, pl.ds(q * NBEAM, NBEAM), :] = lax.dot_general(
            chosen[:, q * STATIONS : (q + 1) * STATIONS], spread, NN,
            preferred_element_type=jnp.float32,
        ).astype(jnp.bfloat16)


def form_beams(frames, l, mine, weight_ref, beam_ref):
    spectra = jnp.concatenate([mine[frame][...].reshape(INPUTS, NL) for frame in frames], axis=1)
    sums = lax.dot_general(weight_ref[l], spectra, NN, preferred_element_type=jnp.float32)
    for n, frame in enumerate(frames):
        straight = sums[:NBEAM, n * NL : (n + 1) * NL]
        crossed = sums[NBEAM:, n * NL : (n + 1) * NL]
        crossed = jnp.concatenate([-crossed[:, AVG:], crossed[:, :AVG]], axis=1)
        voltage = straight + crossed
        power = (voltage * voltage).T
        beam_ref[l, frame] = power[:AVG] + power[AVG:]


def correlator_kernel(
    own_ref, coefs_ref, first_ref, twid_ref, second_ref, order_ref, table_ref, index_ref,
    vis_ref, beam_ref,
    past_ref, coef_ref, rows_ref, send_ref,
    mine0, mine1, mine2, mine3, left0, left1, left2, left3,
    right0, right1, right2, right3, far0, far1, far2, far3,
    acc_ref, weight_ref,
    past_send, past_recv, out_sem, in_sem, ysend_sem, yin_sem,
):
    section = lax.axis_index("section")
    chan = lax.axis_index("chan")
    x, z, core = chan // XBLOCK, (chan % XBLOCK) // NCORE, chan % NCORE
    right, left = (section + 1) % NSEC, (section + NSEC - 1) % NSEC
    mine, lefts = (mine0, mine1, mine2, mine3), (left0, left1, left2, left3)
    rights, fars = (right0, right1, right2, right3), (far0, far1, far2, far3)

    barrier = pltpu.get_barrier_semaphore()

    @pl.loop(1, NCHAN)
    def _(k):
        pl.semaphore_signal(
            barrier, inc=1, device_id=(section, (chan + k) % NCHAN), device_id_type=MESH
        )

    for other in (left, right):
        pl.semaphore_signal(barrier, inc=1, device_id=(other, chan), device_id_type=MESH)

    for a in range(NA):
        coef_ref[pl.ds(a, TAPS, stride=NA), :] = coefs_ref[:, a * NL : (a + 1) * NL]

    def sources(q, i, t):
        return own_ref[q, i, t] if t >= 0 else past_ref[t + TAPS - 1, q, i]

    def fft(frame, lower, upper):
        transform(
            frame, lower, upper, sources, coef_ref, first_ref, twid_ref, second_ref, rows_ref
        )

    def halo(t):
        return pltpu.make_async_remote_copy(
            src_ref=own_ref.at[:, :, t + FRAMES],
            dst_ref=past_ref.at[t + TAPS - 1],
            send_sem=past_send.at[t + TAPS - 1],
            recv_sem=past_recv.at[t + TAPS - 1],
            device_id=(right, chan),
            device_id_type=MESH,
        )

    def halo_wait(t):
        halo(t).wait_recv()

        @pl.when(section == 0)
        def _():
            past_ref[t + TAPS - 1] = jnp.zeros(past_ref.shape[1:], jnp.bfloat16)

    def piece(frame, dx, j):
        dz, dc = j // NCORE, j % NCORE
        peer = ((x + dx) % NX) * XBLOCK + ((z + dz) % NZ) * NCORE + (core + dc) % NCORE
        return pltpu.make_async_remote_copy(
            src_ref=send_ref.at[frame, peer],
            dst_ref=mine[frame].at[chan],
            send_sem=out_sem.at[frame, dx],
            recv_sem=in_sem.at[frame, dx],
            device_id=(section, peer),
            device_id_type=MESH,
        )

    def scatter(frame):
        send_ref[frame] = rows_ref[...].astype(jnp.bfloat16).reshape(NCHAN, LOCAL, NL)
        pltpu.make_async_copy(
            send_ref.at[frame, chan], mine[frame].at[chan], in_sem.at[frame, 0]
        ).start()
        for dx in range(NX):

            @pl.loop(1 if dx == 0 else 0, XBLOCK)
            def _(j):
                piece(frame, dx, j).start()

    def ycopy(source, target, dx, peer, frame, slot):
        part = pl.ds(((x + NX - dx) % NX) * XBLOCK, XBLOCK)
        return pltpu.make_async_remote_copy(
            src_ref=source[frame].at[part],
            dst_ref=target[frame].at[part],
            send_sem=ysend_sem.at[frame, dx, slot],
            recv_sem=yin_sem.at[frame, dx, slot],
            device_id=(peer, chan),
            device_id_type=MESH,
        )

    def to_right(frame, dx):
        return ycopy(mine, lefts, dx, right, frame, 0)

    def to_left(frame, dx):
        return ycopy(mine, rights, dx, left, frame, 1)

    def onward(frame, dx):
        if (frame, dx) in BY_RIGHT:
            return ycopy(lefts, fars, dx, right, frame, 2)
        return ycopy(rights, fars, dx, left, frame, 2)

    def forward(frame, dx):
        part = mine[frame].at[pl.ds(((x + NX - dx) % NX) * XBLOCK, XBLOCK)]
        pltpu.make_async_copy(part, part, in_sem.at[frame, dx]).wait()
        to_left(frame, dx).start()
        to_right(frame, dx).start()

    def relay(frame, dx):
        (to_right if (frame, dx) in BY_RIGHT else to_left)(frame, dx).wait_recv()
        onward(frame, dx).start()

    def near_wait(frame):
        for dx in range(NX):
            (to_left if (frame, dx) in BY_RIGHT else to_right)(frame, dx).wait_recv()

    def far_wait(frame):
        for dx in range(NX):
            onward(frame, dx).wait_recv()

    def products(buffers, first=False, last=False):
        @pl.loop(0, ITEMS)
        def _(item):
            multiply(
                item, buffers, acc_ref, vis_ref, order_ref, section * ITEMS, first, last
            )

    def weights(l):
        make_weights(l, table_ref, index_ref, weight_ref)

    def beams(frames, l):
        form_beams(frames, l, mine, weight_ref, beam_ref)

    half = LOCAL // 2
    fft(3, 0, LOCAL)
    pl.semaphore_wait(barrier, NCHAN + 1)
    for t in (-1, -2, -3):
        halo(t).start()
    scatter(3)
    forward(3, 0)
    weights(0)
    forward(3, 1)
    weights(1)
    forward(3, 2)
    relay(3, 0)
    forward(3, 3)
    relay(3, 1)
    halo_wait(-1)
    fft(2, 0, half)
    relay(3, 2)
    fft(2, half, LOCAL)
    scatter(2)
    relay(3, 3)
    forward(2, 0)
    forward(2, 1)
    relay(2, 0)
    halo_wait(-2)
    fft(1, 0, half)
    forward(2, 2)
    relay(2, 1)
    fft(1, half, LOCAL)
    scatter(1)
    forward(2, 3)
    relay(2, 2)
    forward(1, 0)
    relay(2, 3)
    halo_wait(-3)
    fft(0, 0, half)
    forward(1, 1)
    relay(1, 0)
    fft(0, half, LOCAL)
    scatter(0)
    forward(1, 2)
    relay(1, 1)
    near_wait(3)
    products((mine3, left3, right3), first=True)
    forward(1, 3)
    relay(1, 2)
    beams((3, 2), 0)
    forward(0, 0)
    relay(1, 3)
    beams((3, 2), 1)
    forward(0, 1)
    relay(0, 0)
    far_wait(3)
    near_wait(2)
    products((far3, mine2, left2, right2))
    forward(0, 2)
    relay(0, 1)
    far_wait(2)
    near_wait(1)
    products((far2, mine1, left1, right1))
    forward(0, 3)
    relay(0, 2)
    beams((1, 0), 0)
    relay(0, 3)
    beams((1, 0), 1)
    far_wait(1)
    near_wait(0)
    products((far1, mine0, left0, right0))
    far_wait(0)
    products((far0,), last=True)

    for t in (-1, -2, -3):
        halo(t).wait_send()
    for frame in range(FRAMES):
        for dx in range(NX):
            for copy in (to_right, to_left, onward):
                copy(frame, dx).wait_send()
            sent = send_ref.at[frame, pl.ds(0, XBLOCK - 1 if dx == 0 else XBLOCK)]
            pltpu.make_async_copy(sent, sent, out_sem.at[frame, dx]).wait()


def shards(voltages, coefficients, tile_order, steer_table, beam_index):
    vmem = pl.BlockSpec(memory_space=pltpu.VMEM)
    smem = pl.BlockSpec(memory_space=pltpu.SMEM)
    visibility, beam_power = pl.pallas_call(
        correlator_kernel,
        out_shape=(
            jax.ShapeDtypeStruct((1, ITEMS, 2, TB, TB), jnp.float32),
            jax.ShapeDtypeStruct((2, FRAMES, AVG, NBEAM), jnp.float32),
        ),
        in_specs=[vmem, vmem, vmem, vmem, vmem, smem, vmem, vmem],
        out_specs=(vmem, vmem),
        scratch_shapes=[
            pltpu.VMEM((TAPS - 1, 2, LOCAL, NA, NL), jnp.bfloat16),
            pltpu.VMEM((TAPS * NA, NL), jnp.float32),
            pltpu.VMEM((NCHAN * LOCAL, NL), jnp.float32),
            pltpu.VMEM((FRAMES, NCHAN, LOCAL, NL), jnp.bfloat16),
        ]
        + [pltpu.VMEM((NCHAN, LOCAL, NL), jnp.bfloat16)] * (4 * FRAMES)
        + [
            pltpu.VMEM((ITEMS, 2 * TB, TB), jnp.float32),
            pltpu.VMEM((2, 2 * NBEAM, INPUTS), jnp.bfloat16),
            pltpu.SemaphoreType.DMA((TAPS - 1,)),
            pltpu.SemaphoreType.DMA((TAPS - 1,)),
            pltpu.SemaphoreType.DMA((FRAMES, NX)),
            pltpu.SemaphoreType.DMA((FRAMES, NX)),
            pltpu.SemaphoreType.DMA((FRAMES, NX, 3)),
            pltpu.SemaphoreType.DMA((FRAMES, NX, 3)),
        ],
        compiler_params=pltpu.CompilerParams(
            collective_id=0, has_side_effects=True, vmem_limit_bytes=48 * 1024 * 1024
        ),
        name="correlator",
    )(
        voltages.reshape(2, LOCAL, FRAMES, NA, NL),
        coefficients,
        *tables(),
        tile_order,
        steer_table.reshape(NBEAM, 2 * STATIONS),
        beam_index.reshape(1, NBEAM),
    )
    return visibility, jnp.transpose(beam_power, (0, 3, 1, 2))


def solution(mesh):
    placed = (P(None, "chan", "section", None), P(), P("chan", None), P(), P(None, "chan"))
    return jax.shard_map(
        shards,
        mesh=mesh,
        in_specs=placed,
        out_specs=(P("chan", "section", None, None, None), P(None, None, "section", "chan")),
        check_vma=False,
    )
```

```python
import jax
import jax.numpy as jnp
import ml_dtypes
import numpy as np
from jax import lax
from jax.experimental import pallas as pl
from jax.experimental.pallas import tpu as pltpu
from jax.sharding import PartitionSpec as P

NSEC = 4
FRAMES = 4
CHUNKS = (3, 2, 4, 1)
HALOS = (-1, 4, -2)
NX, NZ, NCORE = 4, 8, 2
NCHAN = NX * NZ * NCORE
XBLOCK = NZ * NCORE
LOCAL = 16
NCH = 4096
TAPS = 4
NA = 32
NL = 128
AVG = 64
TB = 128
ITEMS = 9
UNROLL = 8
NBEAM = 256
STATIONS = 512
INPUTS = 1024
MEAN = 1.0 / 1024.0
NT = (((1,), (1,)), ((), ()))
NN = (((1,), (0,)), ((), ()))
TN = (((0,), (0,)), ((), ()))
MESH = pl.DeviceIdType.MESH
BY_RIGHT = ((1, 1), (1, 3), (2, 1), (2, 3), (4, 1), (4, 3))


def split_np(table):
    high = table.astype(ml_dtypes.bfloat16)
    low = (table - high.astype(np.float64)).astype(ml_dtypes.bfloat16)
    return high, low


def tables():
    c = np.arange(NA)
    angle = 2.0 * np.pi / NA * ((c[:, None] * c[None, :]) % NA)
    cosine, sine = np.cos(angle), np.sin(angle)
    first = np.block([[cosine, sine], [-sine, cosine]])
    high, low = split_np(first)
    first = np.concatenate([high, low, high], axis=1)
    channel = np.arange(AVG)
    lane = np.arange(NL)
    angle = 2.0 * np.pi / NCH * ((channel[:, None] * lane[None, :]) % NCH)
    twiddle = np.stack([np.cos(angle), np.sin(angle)]).astype(np.float32)
    group = np.arange(NCHAN)
    angle = 2.0 * np.pi / NCHAN * ((group[:, None] * lane[None, :]) % NCHAN)
    cosine, sine = np.cos(angle), np.sin(angle)
    second = np.concatenate([cosine, sine], axis=1)
    high, low = split_np(second)
    second = np.concatenate([high, low, high], axis=1)
    return jnp.asarray(first), jnp.asarray(twiddle), jnp.asarray(second)


def split(value):
    high = value.astype(jnp.bfloat16)
    return high, (value - high.astype(jnp.float32)).astype(jnp.bfloat16)


def transform(frame, lower, upper, sources, coef_ref, first_ref, twid_ref, second_ref, rows_ref):
    @pl.loop(lower, upper, step=UNROLL)
    def _(start):
        columns = []
        for u in range(UNROLL):
            parts = []
            for q in range(2):
                total = None
                for p in range(TAPS):
                    term = coef_ref[pl.ds(p * NA, NA), :] * sources(q, start + u, frame - p).astype(jnp.float32)
                    total = term if total is None else total + term
                parts.append(total)
            columns.append(jnp.concatenate(parts, axis=0))
        high, low = split(jnp.concatenate(columns, axis=1))
        section_one = lax.dot_general(
            first_ref[...],
            jnp.concatenate([high, high, low], axis=0),
            NN,
            preferred_element_type=jnp.float32,
        )
        cosine, sine = twid_ref[0], twid_ref[1]
        turned = []
        for u in range(UNROLL):
            real = section_one[:NA, u * NL : (u + 1) * NL]
            imag = section_one[NA:, u * NL : (u + 1) * NL]
            real = jnp.concatenate([real, real], axis=0)
            imag = jnp.concatenate([imag, imag], axis=0)
            real, imag = real * cosine + imag * sine, imag * cosine - real * sine
            rows = jnp.concatenate(
                [jnp.concatenate([real, imag], axis=1), jnp.concatenate([imag, -real], axis=1)], axis=0
            )
            high, low = split(rows)
            turned.append(jnp.concatenate([high, high, low], axis=1))
        section_two = lax.dot_general(
            second_ref[...],
            jnp.concatenate(turned, axis=0),
            NT,
            preferred_element_type=jnp.float32,
        )
        for u in range(UNROLL):
            rows_ref[pl.ds(start + u, NCHAN, stride=LOCAL), :] = section_two[
                :, u * NL : (u + 1) * NL
            ]


def relayout(volts_ref, own_ref, spread_ref):
    @pl.loop(0, 2 * LOCAL, step=2)
    def _(n):
        for u in range(2):
            q, i = lax.div(n, LOCAL), lax.rem(n, LOCAL) + u
            samples = volts_ref[q, i].astype(jnp.float32)
            for a in range(NA):
                spread_ref[u, pl.ds(a, FRAMES, stride=NA), :] = samples[:, a * NL : (a + 1) * NL]
            own_ref[q, i] = spread_ref[u].reshape(FRAMES, NA, NL).astype(jnp.bfloat16)


def tile(buffer, index):
    return buffer[pl.ds(index * (TB // LOCAL), TB // LOCAL)].reshape(TB, NL)


def turned_tile(buffer, index):
    part = tile(buffer, index)
    return jnp.concatenate([part[:, AVG:], -part[:, :AVG]], axis=1)


def multiply(item, buffers, acc_ref, vis_ref, order_ref, offset, first, last):
    n = order_ref[0, offset + item]
    a = 0
    for k in range(1, INPUTS // TB):
        a = a + (n >= k * (k + 1) // 2).astype(jnp.int32)
    b = n - a * (a + 1) // 2
    straight = jnp.concatenate([tile(buffer, a) for buffer in buffers], axis=1)
    turned = jnp.concatenate([turned_tile(buffer, a) for buffer in buffers], axis=1)
    gram = lax.dot_general(
        jnp.concatenate([straight, turned], axis=0),
        jnp.concatenate([tile(buffer, b) for buffer in buffers], axis=1),
        NT,
        preferred_element_type=jnp.float32,
    )
    if not first:
        gram = gram + acc_ref[item]
    if last:
        vis_ref[0, item] = (gram * MEAN).reshape(2, TB, TB)
    else:
        acc_ref[item] = gram


def make_weights(l, table_ref, index_ref, weight_ref):
    picked = (
        lax.broadcasted_iota(jnp.int32, (NBEAM, NBEAM), 0) == index_ref[...]
    ).astype(jnp.float32).astype(jnp.bfloat16)
    chosen = lax.dot_general(
        picked,
        jnp.concatenate([table_ref[:, 0, :], table_ref[:, 1, :]], axis=1),
        TN,
        preferred_element_type=jnp.float32,
    ).astype(jnp.bfloat16)
    spread = (
        lax.broadcasted_iota(jnp.int32, (STATIONS, INPUTS), 1)
        == 2 * lax.broadcasted_iota(jnp.int32, (STATIONS, INPUTS), 0) + l
    ).astype(jnp.float32).astype(jnp.bfloat16)
    for q in range(2):
        weight_ref[l, pl.ds(q * NBEAM, NBEAM), :] = lax.dot_general(
            chosen[:, q * STATIONS : (q + 1) * STATIONS], spread, NN,
            preferred_element_type=jnp.float32,
        ).astype(jnp.bfloat16)


def form_beams(frames, l, sources, weight_ref, beam_ref):
    spectra = jnp.concatenate([sources[frame][...].reshape(INPUTS, NL) for frame in frames], axis=1)
    sums = lax.dot_general(weight_ref[l], spectra, NN, preferred_element_type=jnp.float32)
    for n, frame in enumerate(frames):
        straight = sums[:NBEAM, n * NL : (n + 1) * NL]
        crossed = sums[NBEAM:, n * NL : (n + 1) * NL]
        crossed = jnp.concatenate([-crossed[:, AVG:], crossed[:, :AVG]], axis=1)
        voltage = straight + crossed
        power = (voltage * voltage).T
        beam_ref[l, frame] = power[:AVG] + power[AVG:]


def correlator_kernel(
    volts_hbm, coefs_hbm, first_hbm, twid_hbm, second_hbm, order_hbm, table_hbm, index_hbm,
    vis_ref, beam_ref,
    volts_ref, coefs_ref, first_ref, twid_ref, second_ref, order_ref, table_ref, index_ref,
    own_ref, spread_ref, past_ref, next_ref, coef_ref, rows_ref, send_ref,
    mine1, mine2, mine3, mine4, left1, left2, left3, left4,
    right1, right2, right3, right4, far1, far2, far3, far4,
    acc_ref, weight_ref,
    load_sem, halo_send, halo_recv, out_sem, in_sem, ysend_sem, yin_sem,
):
    section = lax.axis_index("section")
    chan = lax.axis_index("chan")
    x, z, core = chan // XBLOCK, (chan % XBLOCK) // NCORE, chan % NCORE
    right, left = (section + 1) % NSEC, (section + NSEC - 1) % NSEC
    mine = {1: mine1, 2: mine2, 3: mine3, 4: mine4}
    lefts = {1: left1, 2: left2, 3: left3, 4: left4}
    rights = {1: right1, 2: right2, 3: right3, 4: right4}
    fars = {1: far1, 2: far2, 3: far3, 4: far4}

    arrays = (
        (volts_hbm, volts_ref), (coefs_hbm, coefs_ref), (first_hbm, first_ref),
        (twid_hbm, twid_ref), (second_hbm, second_ref), (order_hbm, order_ref),
        (table_hbm, table_ref), (index_hbm, index_ref),
    )
    loads = [
        pltpu.make_async_copy(source, target, load_sem.at[n])
        for n, (source, target) in enumerate(arrays)
    ]
    for load in loads:
        load.start()

    barrier = pltpu.get_barrier_semaphore()

    @pl.loop(1, NCHAN)
    def _(k):
        pl.semaphore_signal(
            barrier, inc=1, device_id=(section, (chan + k) % NCHAN), device_id_type=MESH
        )

    for other in (left, right):
        pl.semaphore_signal(barrier, inc=1, device_id=(other, chan), device_id_type=MESH)

    def sources(q, i, t):
        if t < 0:
            return past_ref[t + 2, q, i]
        return own_ref[q, i, t] if t < FRAMES else next_ref[q, i]

    def spread_coefficients():
        keep = jnp.where(section < NSEC - 1, 1.0, 0.0)
        for a in range(NA):
            coef_ref[0, pl.ds(a, TAPS, stride=NA), :] = coefs_ref[:, a * NL : (a + 1) * NL]
        coef_ref[1, :NA] = coef_ref[0, :NA]
        coef_ref[1, NA:] = coef_ref[0, NA:] * keep

    def fft(frame):
        transform(
            frame, 0, LOCAL, sources, coef_ref.at[1 if frame == FRAMES else 0],
            first_ref, twid_ref, second_ref, rows_ref,
        )

    def halo(t):
        if t == FRAMES:
            source, target, peer = own_ref.at[:, :, 0], next_ref, left
        else:
            source, target, peer = own_ref.at[:, :, t + FRAMES], past_ref.at[t + 2], right
        return pltpu.make_async_remote_copy(
            src_ref=source,
            dst_ref=target,
            send_sem=halo_send.at[HALOS.index(t)],
            recv_sem=halo_recv.at[HALOS.index(t)],
            device_id=(peer, chan),
            device_id_type=MESH,
        )

    def halo_wait(t):
        halo(t).wait_recv()
        if t < 0:

            @pl.when(section == 0)
            def _():
                past_ref[t + 2] = jnp.zeros(past_ref.shape[1:], jnp.bfloat16)

    def piece(frame, dx, j):
        dz, dc = lax.div(j, NCORE), lax.rem(j, NCORE)
        peer = (
            lax.rem(x + dx, NX) * XBLOCK + lax.rem(z + dz, NZ) * NCORE + lax.rem(core + dc, NCORE)
        )
        return pltpu.make_async_remote_copy(
            src_ref=send_ref.at[frame - 1, peer],
            dst_ref=mine[frame].at[chan],
            send_sem=out_sem.at[frame - 1, dx],
            recv_sem=in_sem.at[frame - 1, dx],
            device_id=(section, peer),
            device_id_type=MESH,
        )

    def ready(frame):
        send_ref[frame - 1] = rows_ref[...].astype(jnp.bfloat16).reshape(NCHAN, LOCAL, NL)
        pltpu.make_async_copy(
            send_ref.at[frame - 1, chan], mine[frame].at[chan], in_sem.at[frame - 1, 0]
        ).start()

    def scatter(frame, dx):
        @pl.loop(1 if dx == 0 else 0, XBLOCK)
        def _(j):
            piece(frame, dx, j).start()

    def ycopy(source, target, dx, peer, frame, slot):
        part = pl.ds(((x + NX - dx) % NX) * XBLOCK, XBLOCK)
        return pltpu.make_async_remote_copy(
            src_ref=source[frame].at[part],
            dst_ref=target[frame].at[part],
            send_sem=ysend_sem.at[frame - 1, dx, slot],
            recv_sem=yin_sem.at[frame - 1, dx, slot],
            device_id=(peer, chan),
            device_id_type=MESH,
        )

    def to_right(frame, dx):
        return ycopy(mine, lefts, dx, right, frame, 0)

    def to_left(frame, dx):
        return ycopy(mine, rights, dx, left, frame, 1)

    def onward(frame, dx):
        if (frame, dx) in BY_RIGHT:
            return ycopy(lefts, fars, dx, right, frame, 2)
        return ycopy(rights, fars, dx, left, frame, 2)

    def forward(frame, dx):
        part = mine[frame].at[pl.ds(((x + NX - dx) % NX) * XBLOCK, XBLOCK)]
        pltpu.make_async_copy(part, part, in_sem.at[frame - 1, dx]).wait()
        to_left(frame, dx).start()
        to_right(frame, dx).start()

    def relay(frame, dx):
        (to_right if (frame, dx) in BY_RIGHT else to_left)(frame, dx).wait_recv()
        onward(frame, dx).start()

    def near_wait(frame):
        for dx in range(NX):
            (to_left if (frame, dx) in BY_RIGHT else to_right)(frame, dx).wait_recv()

    def far_wait(frame):
        for dx in range(NX):
            onward(frame, dx).wait_recv()

    def products(buffers, first=False, last=False):
        for item in range(ITEMS):
            multiply(
                item, buffers, acc_ref, vis_ref, order_ref, section * ITEMS, first, last
            )

    def weights(l):
        make_weights(l, table_ref, index_ref, weight_ref)

    def beams(frames, l):
        form_beams(frames, l, {**mine, 0: left4}, weight_ref, beam_ref)

    loads[0].wait()
    relayout(volts_ref, own_ref, spread_ref)
    for load in loads[1:]:
        load.wait()
    spread_coefficients()
    pl.semaphore_wait(barrier, NCHAN + 1)
    for t in (-1, FRAMES, -2):
        halo(t).start()
    fft(3)
    ready(3)
    scatter(3, 0)
    scatter(3, 1)
    scatter(3, 2)
    scatter(3, 3)
    forward(3, 0)
    forward(3, 1)
    forward(3, 2)
    forward(3, 3)
    halo_wait(-1)
    fft(2)
    ready(2)
    scatter(2, 0)
    scatter(2, 1)
    relay(3, 0)
    scatter(2, 2)
    scatter(2, 3)
    relay(3, 1)
    halo_wait(FRAMES)
    fft(4)
    ready(4)
    forward(2, 0)
    relay(3, 2)
    scatter(4, 0)
    forward(2, 1)
    scatter(4, 1)
    relay(3, 3)
    forward(2, 2)
    scatter(4, 2)
    scatter(4, 3)
    forward(2, 3)
    halo_wait(-2)
    fft(1)
    ready(1)
    forward(4, 0)
    scatter(1, 0)
    scatter(1, 1)
    forward(4, 1)
    relay(2, 0)
    scatter(1, 2)
    scatter(1, 3)
    forward(4, 2)
    relay(2, 1)
    forward(4, 3)
    weights(0)
    forward(1, 0)
    relay(2, 2)
    weights(1)
    forward(1, 1)
    relay(2, 3)
    forward(1, 2)
    relay(4, 0)
    forward(1, 3)
    relay(4, 1)
    near_wait(3)
    products((mine3, left3, right3), first=True)
    relay(4, 2)
    beams((3, 2), 0)
    relay(4, 3)
    beams((3, 2), 1)
    far_wait(3)
    near_wait(2)
    products((far3, mine2, left2, right2))
    relay(1, 0)
    near_wait(4)
    beams((1, 0), 0)
    relay(1, 1)
    beams((1, 0), 1)
    relay(1, 2)
    far_wait(2)
    products((far2, mine4, left4, right4))
    relay(1, 3)
    far_wait(4)
    near_wait(1)
    products((far4, mine1, left1, right1))
    far_wait(1)
    products((far1,), last=True)

    for t in (-1, FRAMES, -2):
        halo(t).wait_send()
    for frame in CHUNKS:
        for dx in range(NX):
            for copy in (to_right, to_left, onward):
                copy(frame, dx).wait_send()
            sent = send_ref.at[frame - 1, pl.ds(0, XBLOCK - 1 if dx == 0 else XBLOCK)]
            pltpu.make_async_copy(sent, sent, out_sem.at[frame - 1, dx]).wait()


def shards(voltages, coefficients, tile_order, steer_table, beam_index):
    vmem = pl.BlockSpec(memory_space=pltpu.VMEM)
    hbm = pl.BlockSpec(memory_space=pltpu.HBM)
    first, twiddle, second = tables()
    visibility, beam_power = pl.pallas_call(
        correlator_kernel,
        out_shape=(
            pltpu.VMEM((1, ITEMS, 2, TB, TB), jnp.float32),
            pltpu.VMEM((2, FRAMES, AVG, NBEAM), jnp.float32),
        ),
        in_specs=[hbm] * 8,
        out_specs=(vmem, vmem),
        scratch_shapes=[
            pltpu.VMEM(voltages.shape, voltages.dtype),
            pltpu.VMEM(coefficients.shape, coefficients.dtype),
            pltpu.VMEM(first.shape, first.dtype),
            pltpu.VMEM(twiddle.shape, twiddle.dtype),
            pltpu.VMEM(second.shape, second.dtype),
            pltpu.SMEM(tile_order.shape, tile_order.dtype),
            pltpu.VMEM(steer_table.shape, steer_table.dtype),
            pltpu.VMEM((1, NBEAM), beam_index.dtype),
            pltpu.VMEM((2, LOCAL, FRAMES, NA, NL), jnp.bfloat16),
            pltpu.VMEM((2, FRAMES * NA, NL), jnp.float32),
            pltpu.VMEM((2, 2, LOCAL, NA, NL), jnp.bfloat16),
            pltpu.VMEM((2, LOCAL, NA, NL), jnp.bfloat16),
            pltpu.VMEM((2, TAPS * NA, NL), jnp.float32),
            pltpu.VMEM((NCHAN * LOCAL, NL), jnp.float32),
            pltpu.VMEM((FRAMES, NCHAN, LOCAL, NL), jnp.bfloat16),
        ]
        + [pltpu.VMEM((NCHAN, LOCAL, NL), jnp.bfloat16)] * (4 * FRAMES)
        + [
            pltpu.VMEM((ITEMS, 2 * TB, TB), jnp.float32),
            pltpu.VMEM((2, 2 * NBEAM, INPUTS), jnp.bfloat16),
            pltpu.SemaphoreType.DMA((8,)),
            pltpu.SemaphoreType.DMA((3,)),
            pltpu.SemaphoreType.DMA((3,)),
            pltpu.SemaphoreType.DMA((FRAMES, NX)),
            pltpu.SemaphoreType.DMA((FRAMES, NX)),
            pltpu.SemaphoreType.DMA((FRAMES, NX, 3)),
            pltpu.SemaphoreType.DMA((FRAMES, NX, 3)),
        ],
        compiler_params=pltpu.CompilerParams(
            collective_id=0, has_side_effects=True
        ),
        name="correlator",
    )(
        voltages,
        coefficients,
        first,
        twiddle,
        second,
        tile_order,
        steer_table,
        beam_index.reshape(1, NBEAM),
    )
    return visibility, jnp.transpose(beam_power, (0, 3, 1, 2))


def solution(mesh):
    placed = (P(None, "chan", "section", None), P(), P("chan", None), P(), P(None, "chan"))
    return jax.shard_map(
        shards,
        mesh=mesh,
        in_specs=placed,
        out_specs=(P("chan", "section", None, None, None), P(None, None, "section", "chan")),
        check_vma=False,
    )
```

```python
import jax
import jax.numpy as jnp
import ml_dtypes
import numpy as np
from jax import lax
from jax.experimental import pallas as pl
from jax.experimental.pallas import tpu as pltpu
from jax.sharding import PartitionSpec as P

NSEC = 4
FRAMES = 4
CHUNKS = (3, 2, 4, 1)
HALOS = (-1, 4, -2)
NX, NZ, NCORE = 4, 8, 2
NCHAN = NX * NZ * NCORE
XBLOCK = NZ * NCORE
LOCAL = 16
NCH = 4096
TAPS = 4
NA = 32
NL = 128
AVG = 64
TB = 128
ITEMS = 9
UNROLL = 16
ZORDER = (4, 3, 5, 2, 6, 1, 7, 0)
NBEAM = 256
STATIONS = 512
INPUTS = 1024
MEAN = 1.0 / 1024.0
NT = (((1,), (1,)), ((), ()))
NN = (((1,), (0,)), ((), ()))
TN = (((0,), (0,)), ((), ()))
MESH = pl.DeviceIdType.MESH
BY_RIGHT = ((1, 1), (1, 3), (2, 1), (2, 3), (4, 1), (4, 3))


def split_np(table):
    high = table.astype(ml_dtypes.bfloat16)
    low = (table - high.astype(np.float64)).astype(ml_dtypes.bfloat16)
    return high, low


def tables():
    c = np.arange(NA)
    angle = 2.0 * np.pi / NA * ((c[:, None] * c[None, :]) % NA)
    cosine, sine = np.cos(angle), np.sin(angle)
    first = np.block([[cosine, sine], [-sine, cosine]])
    high, low = split_np(first)
    first = np.concatenate([high, low, high], axis=1)
    channel = np.arange(AVG)
    lane = np.arange(NL)
    angle = 2.0 * np.pi / NCH * ((channel[:, None] * lane[None, :]) % NCH)
    twiddle = np.stack([np.cos(angle), np.sin(angle)]).astype(np.float32)
    group = np.arange(NCHAN)
    angle = 2.0 * np.pi / NCHAN * ((group[:, None] * lane[None, :]) % NCHAN)
    cosine, sine = np.cos(angle), np.sin(angle)
    second = np.concatenate([cosine, sine], axis=1)
    high, low = split_np(second)
    second = np.concatenate([high, low, high], axis=1)
    return jnp.asarray(first), jnp.asarray(twiddle), jnp.asarray(second)


def split(value):
    high = value.astype(jnp.bfloat16)
    return high, (value - high.astype(jnp.float32)).astype(jnp.bfloat16)


def transform(frame, lower, upper, sources, coef_ref, first_ref, twid_ref, second_ref, rows_ref):
    @pl.loop(lower, upper, step=UNROLL)
    def _(start):
        columns = []
        for u in range(UNROLL):
            parts = []
            for q in range(2):
                total = None
                for p in range(TAPS):
                    term = coef_ref[pl.ds(p * NA, NA), :] * sources(q, start + u, frame - p).astype(jnp.float32)
                    total = term if total is None else total + term
                parts.append(total)
            columns.append(jnp.concatenate(parts, axis=0))
        high, low = split(jnp.concatenate(columns, axis=1))
        section_one = lax.dot_general(
            first_ref[...],
            jnp.concatenate([high, high, low], axis=0),
            NN,
            preferred_element_type=jnp.float32,
        )
        cosine, sine = twid_ref[0], twid_ref[1]
        turned = []
        for u in range(UNROLL):
            real = section_one[:NA, u * NL : (u + 1) * NL]
            imag = section_one[NA:, u * NL : (u + 1) * NL]
            real = jnp.concatenate([real, real], axis=0)
            imag = jnp.concatenate([imag, imag], axis=0)
            real, imag = real * cosine + imag * sine, imag * cosine - real * sine
            parts = [
                jnp.concatenate(
                    [jnp.concatenate([re, im], axis=1), jnp.concatenate([im, -re], axis=1)], axis=0
                )
                for re, im in zip(split(real), split(imag))
            ]
            turned.append(jnp.concatenate([parts[0], parts[0], parts[1]], axis=1))
        section_two = lax.dot_general(
            second_ref[...],
            jnp.concatenate(turned, axis=0),
            NT,
            preferred_element_type=jnp.float32,
        )
        for u in range(UNROLL):
            rows_ref[pl.ds(start + u, NCHAN, stride=LOCAL), :] = section_two[
                :, u * NL : (u + 1) * NL
            ]


def relayout(volts_ref, own_ref, spread_ref):
    @pl.loop(0, 2 * LOCAL, step=8)
    def _(n):
        for u in range(8):
            q, i = lax.div(n, LOCAL), lax.rem(n, LOCAL) + u
            samples = volts_ref[q, i].astype(jnp.float32)
            for a in range(NA):
                spread_ref[u, pl.ds(a, FRAMES, stride=NA), :] = samples[:, a * NL : (a + 1) * NL]
            own_ref[q, i] = spread_ref[u].reshape(FRAMES, NA, NL).astype(jnp.bfloat16)


def tile(buffer, index):
    return buffer[pl.ds(index * (TB // LOCAL), TB // LOCAL)].reshape(TB, NL)


def turned_tile(buffer, index):
    part = tile(buffer, index)
    return jnp.concatenate([part[:, AVG:], -part[:, :AVG]], axis=1)


def multiply(item, buffers, acc_ref, vis_ref, order_ref, offset, first, last):
    n = order_ref[0, offset + item]
    a = 0
    for k in range(1, INPUTS // TB):
        a = a + (n >= k * (k + 1) // 2).astype(jnp.int32)
    b = n - a * (a + 1) // 2
    straight = jnp.concatenate([tile(buffer, a) for buffer in buffers], axis=1)
    turned = jnp.concatenate([turned_tile(buffer, a) for buffer in buffers], axis=1)
    gram = lax.dot_general(
        jnp.concatenate([straight, turned], axis=0),
        jnp.concatenate([tile(buffer, b) for buffer in buffers], axis=1),
        NT,
        preferred_element_type=jnp.float32,
    )
    if not first:
        gram = gram + acc_ref[item]
    if last:
        vis_ref[0, item] = (gram * MEAN).reshape(2, TB, TB)
    else:
        acc_ref[item] = gram


def make_weights(l, table_ref, index_ref, weight_ref):
    picked = (
        lax.broadcasted_iota(jnp.int32, (NBEAM, NBEAM), 0) == index_ref[...]
    ).astype(jnp.float32).astype(jnp.bfloat16)
    chosen = lax.dot_general(
        picked,
        jnp.concatenate([table_ref[:, 0, :], table_ref[:, 1, :]], axis=1),
        TN,
        preferred_element_type=jnp.float32,
    ).astype(jnp.bfloat16)
    spread = (
        lax.broadcasted_iota(jnp.int32, (STATIONS, INPUTS), 1)
        == 2 * lax.broadcasted_iota(jnp.int32, (STATIONS, INPUTS), 0) + l
    ).astype(jnp.float32).astype(jnp.bfloat16)
    for q in range(2):
        weight_ref[l, pl.ds(q * NBEAM, NBEAM), :] = lax.dot_general(
            chosen[:, q * STATIONS : (q + 1) * STATIONS], spread, NN,
            preferred_element_type=jnp.float32,
        ).astype(jnp.bfloat16)


def form_beams(frames, l, sources, weight_ref, beam_ref):
    spectra = jnp.concatenate([sources[frame][...].reshape(INPUTS, NL) for frame in frames], axis=1)
    sums = lax.dot_general(weight_ref[l], spectra, NN, preferred_element_type=jnp.float32)
    for n, frame in enumerate(frames):
        straight = sums[:NBEAM, n * NL : (n + 1) * NL]
        crossed = sums[NBEAM:, n * NL : (n + 1) * NL]
        crossed = jnp.concatenate([-crossed[:, AVG:], crossed[:, :AVG]], axis=1)
        voltage = straight + crossed
        power = (voltage * voltage).T
        beam_ref[l, frame] = power[:AVG] + power[AVG:]


def correlator_kernel(
    volts_hbm, coefs_hbm, first_hbm, twid_hbm, second_hbm, order_hbm, table_hbm, index_hbm,
    vis_ref, beam_ref,
    volts_ref, coefs_ref, first_ref, twid_ref, second_ref, order_ref, table_ref, index_ref,
    own_ref, spread_ref, past_ref, next_ref, coef_ref, rows_ref, send_ref,
    mine1, mine2, mine3, mine4, left1, left2, left3, left4,
    right1, right2, right3, right4, far1, far2, far3, far4,
    acc_ref, weight_ref,
    load_sem, halo_send, halo_recv, out_sem, in_sem, ysend_sem, yin_sem,
):
    section = lax.axis_index("section")
    chan = lax.axis_index("chan")
    x, z, core = chan // XBLOCK, (chan % XBLOCK) // NCORE, chan % NCORE
    right, left = (section + 1) % NSEC, (section + NSEC - 1) % NSEC
    mine = {1: mine1, 2: mine2, 3: mine3, 4: mine4}
    lefts = {1: left1, 2: left2, 3: left3, 4: left4}
    rights = {1: right1, 2: right2, 3: right3, 4: right4}
    fars = {1: far1, 2: far2, 3: far3, 4: far4}

    arrays = (
        (volts_hbm, volts_ref), (coefs_hbm, coefs_ref), (first_hbm, first_ref),
        (twid_hbm, twid_ref), (second_hbm, second_ref), (order_hbm, order_ref),
        (table_hbm, table_ref), (index_hbm, index_ref),
    )
    loads = [
        pltpu.make_async_copy(source, target, load_sem.at[n])
        for n, (source, target) in enumerate(arrays)
    ]
    for load in loads:
        load.start()

    barrier = pltpu.get_barrier_semaphore()

    @pl.loop(1, NCHAN)
    def _(k):
        pl.semaphore_signal(
            barrier, inc=1, device_id=(section, (chan + k) % NCHAN), device_id_type=MESH
        )

    for other in (left, right):
        pl.semaphore_signal(barrier, inc=1, device_id=(other, chan), device_id_type=MESH)

    def sources(q, i, t):
        if t < 0:
            return past_ref[t + 2, q, i]
        return own_ref[q, i, t] if t < FRAMES else next_ref[q, i]

    def spread_coefficients():
        keep = jnp.where(section < NSEC - 1, 1.0, 0.0)
        for a in range(NA):
            coef_ref[0, pl.ds(a, TAPS, stride=NA), :] = coefs_ref[:, a * NL : (a + 1) * NL]
        coef_ref[1, :NA] = coef_ref[0, :NA]
        coef_ref[1, NA:] = coef_ref[0, NA:] * keep

    def fft(frame):
        transform(
            frame, 0, LOCAL, sources, coef_ref.at[1 if frame == FRAMES else 0],
            first_ref, twid_ref, second_ref, rows_ref,
        )

    def halo(t):
        if t == FRAMES:
            source, target, peer = own_ref.at[:, :, 0], next_ref, left
        else:
            source, target, peer = own_ref.at[:, :, t + FRAMES], past_ref.at[t + 2], right
        return pltpu.make_async_remote_copy(
            src_ref=source,
            dst_ref=target,
            send_sem=halo_send.at[HALOS.index(t)],
            recv_sem=halo_recv.at[HALOS.index(t)],
            device_id=(peer, chan),
            device_id_type=MESH,
        )

    def halo_wait(t):
        halo(t).wait_recv()
        if t < 0:

            @pl.when(section == 0)
            def _():
                past_ref[t + 2] = jnp.zeros(past_ref.shape[1:], jnp.bfloat16)

    def piece(frame, dx, dz, dc):
        peer = (
            lax.rem(x + dx, NX) * XBLOCK + lax.rem(z + dz, NZ) * NCORE + lax.rem(core + dc, NCORE)
        )
        return pltpu.make_async_remote_copy(
            src_ref=send_ref.at[frame - 1, peer],
            dst_ref=mine[frame].at[chan],
            send_sem=out_sem.at[frame - 1, dx],
            recv_sem=in_sem.at[frame - 1, dx],
            device_id=(section, peer),
            device_id_type=MESH,
        )

    def ready(frame):
        send_ref[frame - 1] = rows_ref[...].astype(jnp.bfloat16).reshape(NCHAN, LOCAL, NL)
        pltpu.make_async_copy(
            send_ref.at[frame - 1, chan], mine[frame].at[chan], in_sem.at[frame - 1, 0]
        ).start()

    def scatter(frame, dx):
        for dz in ZORDER:
            for dc in range(NCORE):
                if (dx, dz, dc) != (0, 0, 0):
                    piece(frame, dx, dz, dc).start()

    def ycopy(source, target, dx, peer, frame, slot):
        part = pl.ds(((x + NX - dx) % NX) * XBLOCK, XBLOCK)
        return pltpu.make_async_remote_copy(
            src_ref=source[frame].at[part],
            dst_ref=target[frame].at[part],
            send_sem=ysend_sem.at[frame - 1, dx, slot],
            recv_sem=yin_sem.at[frame - 1, dx, slot],
            device_id=(peer, chan),
            device_id_type=MESH,
        )

    def to_right(frame, dx):
        return ycopy(mine, lefts, dx, right, frame, 0)

    def to_left(frame, dx):
        return ycopy(mine, rights, dx, left, frame, 1)

    def onward(frame, dx):
        if (frame, dx) in BY_RIGHT:
            return ycopy(lefts, fars, dx, right, frame, 2)
        return ycopy(rights, fars, dx, left, frame, 2)

    def forward(frame, dx):
        part = mine[frame].at[pl.ds(((x + NX - dx) % NX) * XBLOCK, XBLOCK)]
        pltpu.make_async_copy(part, part, in_sem.at[frame - 1, dx]).wait()
        to_left(frame, dx).start()
        to_right(frame, dx).start()

    def relay(frame, dx):
        (to_right if (frame, dx) in BY_RIGHT else to_left)(frame, dx).wait_recv()
        onward(frame, dx).start()

    def near_wait(frame):
        for dx in range(NX):
            (to_left if (frame, dx) in BY_RIGHT else to_right)(frame, dx).wait_recv()

    def far_wait(frame):
        for dx in range(NX):
            onward(frame, dx).wait_recv()

    def products(buffers, first=False, last=False):
        for item in range(ITEMS):
            multiply(
                item, buffers, acc_ref, vis_ref, order_ref, section * ITEMS, first, last
            )

    def weights(l):
        make_weights(l, table_ref, index_ref, weight_ref)

    def beams(frames, l):
        form_beams(frames, l, {**mine, 0: left4}, weight_ref, beam_ref)

    loads[0].wait()
    relayout(volts_ref, own_ref, spread_ref)
    for load in loads[1:]:
        load.wait()
    spread_coefficients()
    pl.semaphore_wait(barrier, NCHAN + 1)
    for t in (-1, FRAMES, -2):
        halo(t).start()
    fft(3)
    ready(3)
    scatter(3, 0)
    scatter(3, 1)
    scatter(3, 2)
    scatter(3, 3)
    forward(3, 0)
    forward(3, 1)
    forward(3, 2)
    forward(3, 3)
    halo_wait(-1)
    fft(2)
    ready(2)
    scatter(2, 0)
    scatter(2, 1)
    scatter(2, 2)
    scatter(2, 3)
    relay(3, 0)
    relay(3, 1)
    halo_wait(FRAMES)
    fft(4)
    ready(4)
    scatter(4, 0)
    scatter(4, 1)
    scatter(4, 2)
    scatter(4, 3)
    relay(3, 2)
    forward(2, 0)
    halo_wait(-2)
    fft(1)
    ready(1)
    scatter(1, 0)
    scatter(1, 1)
    scatter(1, 2)
    scatter(1, 3)
    relay(3, 3)
    forward(2, 1)
    forward(2, 2)
    forward(2, 3)
    relay(2, 0)
    forward(4, 0)
    forward(4, 1)
    relay(2, 1)
    forward(4, 2)
    forward(4, 3)
    relay(2, 2)
    weights(0)
    forward(1, 0)
    relay(2, 3)
    weights(1)
    forward(1, 1)
    relay(4, 0)
    forward(1, 2)
    relay(4, 1)
    forward(1, 3)
    near_wait(3)
    products((mine3, left3, right3), first=True)
    relay(4, 2)
    beams((3, 2), 0)
    relay(4, 3)
    beams((3, 2), 1)
    far_wait(3)
    near_wait(2)
    products((far3, mine2, left2, right2))
    relay(1, 0)
    near_wait(4)
    beams((1, 0), 0)
    relay(1, 1)
    beams((1, 0), 1)
    relay(1, 2)
    far_wait(2)
    products((far2, mine4, left4, right4))
    relay(1, 3)
    far_wait(4)
    near_wait(1)
    products((far4, mine1, left1, right1))
    far_wait(1)
    products((far1,), last=True)

    for t in (-1, FRAMES, -2):
        halo(t).wait_send()
    for frame in CHUNKS:
        for dx in range(NX):
            for copy in (to_right, to_left, onward):
                copy(frame, dx).wait_send()
            sent = send_ref.at[frame - 1, pl.ds(0, XBLOCK - 1 if dx == 0 else XBLOCK)]
            pltpu.make_async_copy(sent, sent, out_sem.at[frame - 1, dx]).wait()


def shards(voltages, coefficients, tile_order, steer_table, beam_index):
    vmem = pl.BlockSpec(memory_space=pltpu.VMEM)
    hbm = pl.BlockSpec(memory_space=pltpu.HBM)
    first, twiddle, second = tables()
    visibility, beam_power = pl.pallas_call(
        correlator_kernel,
        out_shape=(
            pltpu.VMEM((1, ITEMS, 2, TB, TB), jnp.float32),
            pltpu.VMEM((2, FRAMES, AVG, NBEAM), jnp.float32),
        ),
        in_specs=[hbm] * 8,
        out_specs=(vmem, vmem),
        scratch_shapes=[
            pltpu.VMEM(voltages.shape, voltages.dtype),
            pltpu.VMEM(coefficients.shape, coefficients.dtype),
            pltpu.VMEM(first.shape, first.dtype),
            pltpu.VMEM(twiddle.shape, twiddle.dtype),
            pltpu.VMEM(second.shape, second.dtype),
            pltpu.SMEM(tile_order.shape, tile_order.dtype),
            pltpu.VMEM(steer_table.shape, steer_table.dtype),
            pltpu.VMEM((1, NBEAM), beam_index.dtype),
            pltpu.VMEM((2, LOCAL, FRAMES, NA, NL), jnp.bfloat16),
            pltpu.VMEM((8, FRAMES * NA, NL), jnp.float32),
            pltpu.VMEM((2, 2, LOCAL, NA, NL), jnp.bfloat16),
            pltpu.VMEM((2, LOCAL, NA, NL), jnp.bfloat16),
            pltpu.VMEM((2, TAPS * NA, NL), jnp.float32),
            pltpu.VMEM((NCHAN * LOCAL, NL), jnp.float32),
            pltpu.VMEM((FRAMES, NCHAN, LOCAL, NL), jnp.bfloat16),
        ]
        + [pltpu.VMEM((NCHAN, LOCAL, NL), jnp.bfloat16)] * (4 * FRAMES)
        + [
            pltpu.VMEM((ITEMS, 2 * TB, TB), jnp.float32),
            pltpu.VMEM((2, 2 * NBEAM, INPUTS), jnp.bfloat16),
            pltpu.SemaphoreType.DMA((8,)),
            pltpu.SemaphoreType.DMA((3,)),
            pltpu.SemaphoreType.DMA((3,)),
            pltpu.SemaphoreType.DMA((FRAMES, NX)),
            pltpu.SemaphoreType.DMA((FRAMES, NX)),
            pltpu.SemaphoreType.DMA((FRAMES, NX, 3)),
            pltpu.SemaphoreType.DMA((FRAMES, NX, 3)),
        ],
        compiler_params=pltpu.CompilerParams(
            collective_id=0, has_side_effects=True
        ),
        name="correlator",
    )(
        voltages,
        coefficients,
        first,
        twiddle,
        second,
        tile_order,
        steer_table,
        beam_index.reshape(1, NBEAM),
    )
    return visibility, jnp.transpose(beam_power, (0, 3, 1, 2))


def solution(mesh):
    placed = (P(None, "chan", "section", None), P(), P("chan", None), P(), P(None, "chan"))
    return jax.shard_map(
        shards,
        mesh=mesh,
        in_specs=placed,
        out_specs=(P("chan", "section", None, None, None), P(None, None, "section", "chan")),
        check_vma=False,
    )
```

```python
import jax
import jax.numpy as jnp
import ml_dtypes
import numpy as np
from jax import lax
from jax.experimental import pallas as pl
from jax.experimental.pallas import tpu as pltpu
from jax.sharding import PartitionSpec as P

NSEC = 4
FRAMES = 4
CHUNKS = (3, 2, 4, 1)
HALOS = (-1, 4, -2)
NX, NZ, NCORE = 4, 8, 2
NCHAN = NX * NZ * NCORE
XBLOCK = NZ * NCORE
LOCAL = 16
NCH = 4096
TAPS = 4
NA = 32
NL = 128
AVG = 64
TB = 128
ITEMS = 9
UNROLL = 16
ZORDER = (4, 3, 5, 2, 6, 1, 7, 0)
NBEAM = 256
STATIONS = 512
INPUTS = 1024
MEAN = 1.0 / 1024.0
NT = (((1,), (1,)), ((), ()))
NN = (((1,), (0,)), ((), ()))
TN = (((0,), (0,)), ((), ()))
MESH = pl.DeviceIdType.MESH
BY_RIGHT = ((1, 1), (1, 3), (2, 3), (4, 1), (4, 3))


def split_np(table):
    high = table.astype(ml_dtypes.bfloat16)
    low = (table - high.astype(np.float64)).astype(ml_dtypes.bfloat16)
    return high, low


def tables():
    c = np.arange(NA)
    angle = 2.0 * np.pi / NA * ((c[:, None] * c[None, :]) % NA)
    cosine, sine = np.cos(angle), np.sin(angle)
    first = np.block([[cosine, sine], [-sine, cosine]])
    high, low = split_np(first)
    first = np.concatenate([high, low, high], axis=1)
    channel = np.arange(AVG)
    lane = np.arange(NL)
    angle = 2.0 * np.pi / NCH * ((channel[:, None] * lane[None, :]) % NCH)
    twiddle = np.stack([np.cos(angle), np.sin(angle)]).astype(np.float32)
    group = np.arange(NCHAN)
    angle = 2.0 * np.pi / NCHAN * ((group[:, None] * lane[None, :]) % NCHAN)
    cosine, sine = np.cos(angle), np.sin(angle)
    second = np.concatenate([cosine, sine], axis=1)
    high, low = split_np(second)
    second = np.concatenate([high, low, high], axis=1)
    return jnp.asarray(first), jnp.asarray(twiddle), jnp.asarray(second)


def split(value):
    high = value.astype(jnp.bfloat16)
    return high, (value - high.astype(jnp.float32)).astype(jnp.bfloat16)


def transform(frame, lower, upper, sources, coef_ref, first_ref, twid_ref, second_ref, rows_ref):
    @pl.loop(lower, upper, step=UNROLL)
    def _(start):
        columns = []
        for u in range(UNROLL):
            parts = []
            for q in range(2):
                total = None
                for p in range(TAPS):
                    term = coef_ref[pl.ds(p * NA, NA), :] * sources(q, start + u, frame - p).astype(jnp.float32)
                    total = term if total is None else total + term
                parts.append(total)
            columns.append(jnp.concatenate(parts, axis=0))
        high, low = split(jnp.concatenate(columns, axis=1))
        section_one = lax.dot_general(
            first_ref[...],
            jnp.concatenate([high, high, low], axis=0),
            NN,
            preferred_element_type=jnp.float32,
        )
        cosine, sine = twid_ref[0], twid_ref[1]
        turned = []
        for u in range(UNROLL):
            real = section_one[:NA, u * NL : (u + 1) * NL]
            imag = section_one[NA:, u * NL : (u + 1) * NL]
            real = jnp.concatenate([real, real], axis=0)
            imag = jnp.concatenate([imag, imag], axis=0)
            real, imag = real * cosine + imag * sine, imag * cosine - real * sine
            parts = [
                jnp.concatenate(
                    [jnp.concatenate([re, im], axis=1), jnp.concatenate([im, -re], axis=1)], axis=0
                )
                for re, im in zip(split(real), split(imag))
            ]
            turned.append(jnp.concatenate([parts[0], parts[0], parts[1]], axis=1))
        section_two = lax.dot_general(
            second_ref[...],
            jnp.concatenate(turned, axis=0),
            NT,
            preferred_element_type=jnp.float32,
        )
        for u in range(UNROLL):
            rows_ref[pl.ds(start + u, NCHAN, stride=LOCAL), :] = section_two[
                :, u * NL : (u + 1) * NL
            ]


def relayout(volts_ref, own_ref, spread_ref):
    @pl.loop(0, 2 * LOCAL, step=8)
    def _(n):
        for u in range(8):
            q, i = lax.div(n, LOCAL), lax.rem(n, LOCAL) + u
            samples = volts_ref[q, i].astype(jnp.float32)
            for a in range(NA):
                spread_ref[u, pl.ds(a, FRAMES, stride=NA), :] = samples[:, a * NL : (a + 1) * NL]
            own_ref[q, i] = spread_ref[u].reshape(FRAMES, NA, NL).astype(jnp.bfloat16)


def tile(buffer, index):
    return buffer[pl.ds(index * (TB // LOCAL), TB // LOCAL)].reshape(TB, NL)


def turned_tile(buffer, index):
    part = tile(buffer, index)
    return jnp.concatenate([part[:, AVG:], -part[:, :AVG]], axis=1)


def multiply(item, buffers, acc_ref, vis_ref, order_ref, offset, first, last):
    n = order_ref[0, offset + item]
    a = 0
    for k in range(1, INPUTS // TB):
        a = a + (n >= k * (k + 1) // 2).astype(jnp.int32)
    b = n - a * (a + 1) // 2
    straight = jnp.concatenate([tile(buffer, a) for buffer in buffers], axis=1)
    turned = jnp.concatenate([turned_tile(buffer, a) for buffer in buffers], axis=1)
    gram = lax.dot_general(
        jnp.concatenate([straight, turned], axis=0),
        jnp.concatenate([tile(buffer, b) for buffer in buffers], axis=1),
        NT,
        preferred_element_type=jnp.float32,
    )
    if not first:
        gram = gram + acc_ref[item]
    if last:
        vis_ref[0, item] = (gram * MEAN).reshape(2, TB, TB)
    else:
        acc_ref[item] = gram


def make_weights(l, table_ref, index_ref, weight_ref):
    picked = (
        lax.broadcasted_iota(jnp.int32, (NBEAM, NBEAM), 0) == index_ref[...]
    ).astype(jnp.float32).astype(jnp.bfloat16)
    chosen = lax.dot_general(
        picked,
        jnp.concatenate([table_ref[:, 0, :], table_ref[:, 1, :]], axis=1),
        TN,
        preferred_element_type=jnp.float32,
    ).astype(jnp.bfloat16)
    spread = (
        lax.broadcasted_iota(jnp.int32, (STATIONS, INPUTS), 1)
        == 2 * lax.broadcasted_iota(jnp.int32, (STATIONS, INPUTS), 0) + l
    ).astype(jnp.float32).astype(jnp.bfloat16)
    for q in range(2):
        weight_ref[l, pl.ds(q * NBEAM, NBEAM), :] = lax.dot_general(
            chosen[:, q * STATIONS : (q + 1) * STATIONS], spread, NN,
            preferred_element_type=jnp.float32,
        ).astype(jnp.bfloat16)


def form_beams(frames, l, sources, weight_ref, beam_ref):
    spectra = jnp.concatenate([sources[frame][...].reshape(INPUTS, NL) for frame in frames], axis=1)
    sums = lax.dot_general(weight_ref[l], spectra, NN, preferred_element_type=jnp.float32)
    for n, frame in enumerate(frames):
        straight = sums[:NBEAM, n * NL : (n + 1) * NL]
        crossed = sums[NBEAM:, n * NL : (n + 1) * NL]
        crossed = jnp.concatenate([-crossed[:, AVG:], crossed[:, :AVG]], axis=1)
        voltage = straight + crossed
        power = (voltage * voltage).T
        beam_ref[l, frame] = power[:AVG] + power[AVG:]


def correlator_kernel(
    volts_hbm, coefs_hbm, first_hbm, twid_hbm, second_hbm, order_hbm, table_hbm, index_hbm,
    vis_ref, beam_ref,
    volts_ref, coefs_ref, first_ref, twid_ref, second_ref, order_ref, table_ref, index_ref,
    own_ref, spread_ref, past_ref, next_ref, coef_ref, rows_ref, send_ref,
    mine1, mine2, mine3, mine4, left1, left2, left3, left4,
    right1, right2, right3, right4, far1, far2, far3, far4,
    acc_ref, weight_ref,
    load_sem, halo_send, halo_recv, out_sem, in_sem, ysend_sem, yin_sem,
):
    section = lax.axis_index("section")
    chan = lax.axis_index("chan")
    x, z, core = chan // XBLOCK, (chan % XBLOCK) // NCORE, chan % NCORE
    right, left = (section + 1) % NSEC, (section + NSEC - 1) % NSEC
    mine = {1: mine1, 2: mine2, 3: mine3, 4: mine4}
    lefts = {1: left1, 2: left2, 3: left3, 4: left4}
    rights = {1: right1, 2: right2, 3: right3, 4: right4}
    fars = {1: far1, 2: far2, 3: far3, 4: far4}

    arrays = (
        (volts_hbm, volts_ref), (coefs_hbm, coefs_ref), (first_hbm, first_ref),
        (twid_hbm, twid_ref), (second_hbm, second_ref), (order_hbm, order_ref),
        (table_hbm, table_ref), (index_hbm, index_ref),
    )
    loads = [
        pltpu.make_async_copy(source, target, load_sem.at[n])
        for n, (source, target) in enumerate(arrays)
    ]
    for load in loads:
        load.start()

    barrier = pltpu.get_barrier_semaphore()

    @pl.loop(1, NCHAN)
    def _(k):
        pl.semaphore_signal(
            barrier, inc=1, device_id=(section, (chan + k) % NCHAN), device_id_type=MESH
        )

    for other in (left, right):
        pl.semaphore_signal(barrier, inc=1, device_id=(other, chan), device_id_type=MESH)

    def sources(q, i, t):
        if t < 0:
            return past_ref[t + 2, q, i]
        return own_ref[q, i, t] if t < FRAMES else next_ref[q, i]

    def spread_coefficients():
        keep = jnp.where(section < NSEC - 1, 1.0, 0.0)
        for a in range(NA):
            coef_ref[0, pl.ds(a, TAPS, stride=NA), :] = coefs_ref[:, a * NL : (a + 1) * NL]
        coef_ref[1, :NA] = coef_ref[0, :NA]
        coef_ref[1, NA:] = coef_ref[0, NA:] * keep

    def fft(frame):
        transform(
            frame, 0, LOCAL, sources, coef_ref.at[1 if frame == FRAMES else 0],
            first_ref, twid_ref, second_ref, rows_ref,
        )

    def halo(t):
        if t == FRAMES:
            source, target, peer = own_ref.at[:, :, 0], next_ref, left
        else:
            source, target, peer = own_ref.at[:, :, t + FRAMES], past_ref.at[t + 2], right
        return pltpu.make_async_remote_copy(
            src_ref=source,
            dst_ref=target,
            send_sem=halo_send.at[HALOS.index(t)],
            recv_sem=halo_recv.at[HALOS.index(t)],
            device_id=(peer, chan),
            device_id_type=MESH,
        )

    def halo_wait(t):
        halo(t).wait_recv()
        if t < 0:

            @pl.when(section == 0)
            def _():
                past_ref[t + 2] = jnp.zeros(past_ref.shape[1:], jnp.bfloat16)

    def piece(frame, dx, dz, dc):
        peer = (
            lax.rem(x + dx, NX) * XBLOCK + lax.rem(z + dz, NZ) * NCORE + lax.rem(core + dc, NCORE)
        )
        return pltpu.make_async_remote_copy(
            src_ref=send_ref.at[frame - 1, peer],
            dst_ref=mine[frame].at[chan],
            send_sem=out_sem.at[frame - 1, dx],
            recv_sem=in_sem.at[frame - 1, dx],
            device_id=(section, peer),
            device_id_type=MESH,
        )

    def ready(frame):
        send_ref[frame - 1] = rows_ref[...].astype(jnp.bfloat16).reshape(NCHAN, LOCAL, NL)
        pltpu.make_async_copy(
            send_ref.at[frame - 1, chan], mine[frame].at[chan], in_sem.at[frame - 1, 0]
        ).start()

    def scatter(frame, dx):
        for dz in ZORDER:
            for dc in range(NCORE):
                if (dx, dz, dc) != (0, 0, 0):
                    piece(frame, dx, dz, dc).start()

    def ycopy(source, target, dx, peer, frame, slot):
        part = pl.ds(((x + NX - dx) % NX) * XBLOCK, XBLOCK)
        return pltpu.make_async_remote_copy(
            src_ref=source[frame].at[part],
            dst_ref=target[frame].at[part],
            send_sem=ysend_sem.at[frame - 1, dx, slot],
            recv_sem=yin_sem.at[frame - 1, dx, slot],
            device_id=(peer, chan),
            device_id_type=MESH,
        )

    def to_right(frame, dx):
        return ycopy(mine, lefts, dx, right, frame, 0)

    def to_left(frame, dx):
        return ycopy(mine, rights, dx, left, frame, 1)

    def onward(frame, dx):
        if (frame, dx) in BY_RIGHT:
            return ycopy(lefts, fars, dx, right, frame, 2)
        return ycopy(rights, fars, dx, left, frame, 2)

    def forward(frame, dx):
        part = mine[frame].at[pl.ds(((x + NX - dx) % NX) * XBLOCK, XBLOCK)]
        pltpu.make_async_copy(part, part, in_sem.at[frame - 1, dx]).wait()
        to_left(frame, dx).start()
        to_right(frame, dx).start()

    def relay(frame, dx):
        (to_right if (frame, dx) in BY_RIGHT else to_left)(frame, dx).wait_recv()
        onward(frame, dx).start()

    def near_wait(frame):
        for dx in range(NX):
            (to_left if (frame, dx) in BY_RIGHT else to_right)(frame, dx).wait_recv()

    def far_wait(frame):
        for dx in range(NX):
            onward(frame, dx).wait_recv()

    def products(buffers, first=False, last=False):
        for item in range(ITEMS):
            multiply(
                item, buffers, acc_ref, vis_ref, order_ref, section * ITEMS, first, last
            )

    def weights(l):
        make_weights(l, table_ref, index_ref, weight_ref)

    def beams(frames, l):
        form_beams(frames, l, {**mine, 0: left4}, weight_ref, beam_ref)

    loads[0].wait()
    relayout(volts_ref, own_ref, spread_ref)
    for load in loads[1:]:
        load.wait()
    spread_coefficients()
    pl.semaphore_wait(barrier, NCHAN + 1)
    for t in (-1, FRAMES, -2):
        halo(t).start()
    fft(3)
    ready(3)
    scatter(3, 0)
    scatter(3, 1)
    scatter(3, 2)
    scatter(3, 3)
    forward(3, 0)
    forward(3, 1)
    forward(3, 2)
    forward(3, 3)
    halo_wait(-1)
    fft(2)
    ready(2)
    scatter(2, 0)
    scatter(2, 1)
    scatter(2, 2)
    scatter(2, 3)
    relay(3, 0)
    relay(3, 1)
    halo_wait(FRAMES)
    fft(4)
    ready(4)
    scatter(4, 0)
    scatter(4, 1)
    scatter(4, 2)
    scatter(4, 3)
    relay(3, 2)
    forward(2, 0)
    halo_wait(-2)
    fft(1)
    ready(1)
    scatter(1, 0)
    scatter(1, 1)
    scatter(1, 2)
    scatter(1, 3)
    relay(3, 3)
    forward(2, 1)
    forward(2, 2)
    forward(2, 3)
    relay(2, 0)
    forward(4, 0)
    forward(4, 1)
    relay(2, 1)
    forward(4, 2)
    forward(4, 3)
    relay(2, 2)
    weights(0)
    forward(1, 0)
    relay(2, 3)
    weights(1)
    forward(1, 1)
    relay(4, 0)
    forward(1, 2)
    relay(4, 1)
    forward(1, 3)
    near_wait(3)
    products((mine3, left3, right3), first=True)
    relay(4, 2)
    beams((3, 2), 0)
    relay(4, 3)
    beams((3, 2), 1)
    far_wait(3)
    near_wait(2)
    products((far3, mine2, left2, right2))
    relay(1, 0)
    near_wait(4)
    beams((1, 0), 0)
    relay(1, 1)
    beams((1, 0), 1)
    relay(1, 2)
    far_wait(2)
    products((far2, mine4, left4, right4))
    relay(1, 3)
    far_wait(4)
    near_wait(1)
    products((far4, mine1, left1, right1))
    far_wait(1)
    products((far1,), last=True)

    for t in (-1, FRAMES, -2):
        halo(t).wait_send()
    for frame in CHUNKS:
        for dx in range(NX):
            for copy in (to_right, to_left, onward):
                copy(frame, dx).wait_send()
            sent = send_ref.at[frame - 1, pl.ds(0, XBLOCK - 1 if dx == 0 else XBLOCK)]
            pltpu.make_async_copy(sent, sent, out_sem.at[frame - 1, dx]).wait()


def store_kernel(vis_ref, beam_ref, vis_hbm, beam_hbm, sems):
    copies = [
        pltpu.make_async_copy(vis_ref, vis_hbm, sems.at[0]),
        pltpu.make_async_copy(beam_ref, beam_hbm, sems.at[1]),
    ]
    for copy in copies:
        copy.start()
    for copy in copies:
        copy.wait()


def shards(voltages, coefficients, tile_order, steer_table, beam_index):
    vmem = pl.BlockSpec(memory_space=pltpu.VMEM)
    hbm = pl.BlockSpec(memory_space=pltpu.HBM)
    first, twiddle, second = tables()
    visibility, beam_power = pl.pallas_call(
        correlator_kernel,
        out_shape=(
            pltpu.VMEM((1, ITEMS, 2, TB, TB), jnp.float32),
            pltpu.VMEM((2, FRAMES, AVG, NBEAM), jnp.float32),
        ),
        in_specs=[hbm] * 8,
        out_specs=(vmem, vmem),
        scratch_shapes=[
            pltpu.VMEM(voltages.shape, voltages.dtype),
            pltpu.VMEM(coefficients.shape, coefficients.dtype),
            pltpu.VMEM(first.shape, first.dtype),
            pltpu.VMEM(twiddle.shape, twiddle.dtype),
            pltpu.VMEM(second.shape, second.dtype),
            pltpu.SMEM(tile_order.shape, tile_order.dtype),
            pltpu.VMEM(steer_table.shape, steer_table.dtype),
            pltpu.VMEM((1, NBEAM), beam_index.dtype),
            pltpu.VMEM((2, LOCAL, FRAMES, NA, NL), jnp.bfloat16),
            pltpu.VMEM((8, FRAMES * NA, NL), jnp.float32),
            pltpu.VMEM((2, 2, LOCAL, NA, NL), jnp.bfloat16),
            pltpu.VMEM((2, LOCAL, NA, NL), jnp.bfloat16),
            pltpu.VMEM((2, TAPS * NA, NL), jnp.float32),
            pltpu.VMEM((NCHAN * LOCAL, NL), jnp.float32),
            pltpu.VMEM((FRAMES, NCHAN, LOCAL, NL), jnp.bfloat16),
        ]
        + [pltpu.VMEM((NCHAN, LOCAL, NL), jnp.bfloat16)] * (4 * FRAMES)
        + [
            pltpu.VMEM((ITEMS, 2 * TB, TB), jnp.float32),
            pltpu.VMEM((2, 2 * NBEAM, INPUTS), jnp.bfloat16),
            pltpu.SemaphoreType.DMA((8,)),
            pltpu.SemaphoreType.DMA((3,)),
            pltpu.SemaphoreType.DMA((3,)),
            pltpu.SemaphoreType.DMA((FRAMES, NX)),
            pltpu.SemaphoreType.DMA((FRAMES, NX)),
            pltpu.SemaphoreType.DMA((FRAMES, NX, 3)),
            pltpu.SemaphoreType.DMA((FRAMES, NX, 3)),
        ],
        compiler_params=pltpu.CompilerParams(
            collective_id=0, has_side_effects=True
        ),
        name="correlator",
    )(
        voltages,
        coefficients,
        first,
        twiddle,
        second,
        tile_order,
        steer_table,
        beam_index.reshape(1, NBEAM),
    )
    visibility, beam_power = pl.pallas_call(
        store_kernel,
        out_shape=(
            jax.ShapeDtypeStruct(visibility.shape, visibility.dtype),
            jax.ShapeDtypeStruct(beam_power.shape, beam_power.dtype),
        ),
        in_specs=[vmem, vmem],
        out_specs=(hbm, hbm),
        scratch_shapes=[pltpu.SemaphoreType.DMA((2,))],
        compiler_params=pltpu.CompilerParams(vmem_limit_bytes=4 * 1024 * 1024),
        name="store",
    )(visibility, beam_power)
    return visibility, jnp.transpose(beam_power, (0, 3, 1, 2))


def solution(mesh):
    placed = (P(None, "chan", "section", None), P(), P("chan", None), P(), P(None, "chan"))
    return jax.shard_map(
        shards,
        mesh=mesh,
        in_specs=placed,
        out_specs=(P("chan", "section", None, None, None), P(None, None, "section", "chan")),
        check_vma=False,
    )
```

```python
import jax
import jax.numpy as jnp
import ml_dtypes
import numpy as np
from jax import lax
from jax.experimental import pallas as pl
from jax.experimental.pallas import tpu as pltpu
from jax.sharding import PartitionSpec as P

NSEC = 4
FRAMES = 4
CHUNKS = (3, 2, 4, 1)
HALOS = (-1, 4, -2)
NX, NZ, NCORE = 4, 8, 2
NCHAN = NX * NZ * NCORE
XBLOCK = NZ * NCORE
LOCAL = 16
NCH = 4096
TAPS = 4
NA = 32
NL = 128
AVG = 64
TB = 128
ITEMS = 9
UNROLL = 16
ZORDER = (4, 3, 5, 2, 6, 1, 7, 0)
NBEAM = 256
STATIONS = 512
INPUTS = 1024
MEAN = 1.0 / 1024.0
NT = (((1,), (1,)), ((), ()))
NN = (((1,), (0,)), ((), ()))
TN = (((0,), (0,)), ((), ()))
MESH = pl.DeviceIdType.MESH
BY_RIGHT = ((1, 1), (1, 3), (2, 3), (4, 1), (4, 3))


def split_np(table):
    high = table.astype(ml_dtypes.bfloat16)
    low = (table - high.astype(np.float64)).astype(ml_dtypes.bfloat16)
    return high, low


def tables():
    c = np.arange(NA)
    angle = 2.0 * np.pi / NA * ((c[:, None] * c[None, :]) % NA)
    cosine, sine = np.cos(angle), np.sin(angle)
    first = np.block([[cosine, sine], [-sine, cosine]])
    high, low = split_np(first)
    first = np.concatenate([high, low, high], axis=1)
    channel = np.arange(AVG)
    lane = np.arange(NL)
    angle = 2.0 * np.pi / NCH * ((channel[:, None] * lane[None, :]) % NCH)
    twiddle = np.stack([np.cos(angle), np.sin(angle)]).astype(np.float32)
    group = np.arange(NCHAN)
    angle = 2.0 * np.pi / NCHAN * ((group[:, None] * lane[None, :]) % NCHAN)
    cosine, sine = np.cos(angle), np.sin(angle)
    second = np.concatenate([cosine, sine], axis=1)
    high, low = split_np(second)
    second = np.concatenate([high, low, high], axis=1)
    return jnp.asarray(first), jnp.asarray(twiddle), jnp.asarray(second)


def split(value):
    high = value.astype(jnp.bfloat16)
    return high, (value - high.astype(jnp.float32)).astype(jnp.bfloat16)


def transform(frame, lower, upper, sources, coef_ref, first_ref, twid_ref, second_ref, rows_ref):
    @pl.loop(lower, upper, step=UNROLL)
    def _(start):
        columns = []
        for u in range(UNROLL):
            parts = []
            for q in range(2):
                total = None
                for p in range(TAPS):
                    term = coef_ref[pl.ds(p * NA, NA), :] * sources(q, start + u, frame - p).astype(jnp.float32)
                    total = term if total is None else total + term
                parts.append(total)
            columns.append(jnp.concatenate(parts, axis=0))
        high, low = split(jnp.concatenate(columns, axis=1))
        section_one = lax.dot_general(
            first_ref[...],
            jnp.concatenate([high, high, low], axis=0),
            NN,
            preferred_element_type=jnp.float32,
        )
        cosine, sine = twid_ref[0], twid_ref[1]
        turned = []
        for u in range(UNROLL):
            real = section_one[:NA, u * NL : (u + 1) * NL]
            imag = section_one[NA:, u * NL : (u + 1) * NL]
            real = jnp.concatenate([real, real], axis=0)
            imag = jnp.concatenate([imag, imag], axis=0)
            real, imag = real * cosine + imag * sine, imag * cosine - real * sine
            parts = [
                jnp.concatenate(
                    [jnp.concatenate([re, im], axis=1), jnp.concatenate([im, -re], axis=1)], axis=0
                )
                for re, im in zip(split(real), split(imag))
            ]
            turned.append(jnp.concatenate([parts[0], parts[0], parts[1]], axis=1))
        section_two = lax.dot_general(
            second_ref[...],
            jnp.concatenate(turned, axis=0),
            NT,
            preferred_element_type=jnp.float32,
        )
        for u in range(UNROLL):
            rows_ref[pl.ds(start + u, NCHAN, stride=LOCAL), :] = section_two[
                :, u * NL : (u + 1) * NL
            ]


def relayout(volts_ref, own_ref, spread_ref):
    @pl.loop(0, 2 * LOCAL, step=8)
    def _(n):
        for u in range(8):
            q, i = lax.div(n, LOCAL), lax.rem(n, LOCAL) + u
            samples = volts_ref[q, i].astype(jnp.float32)
            for a in range(NA):
                spread_ref[u, pl.ds(a, FRAMES, stride=NA), :] = samples[:, a * NL : (a + 1) * NL]
            own_ref[q, i] = spread_ref[u].reshape(FRAMES, NA, NL).astype(jnp.bfloat16)


def tile(buffer, index):
    return buffer[pl.ds(index * (TB // LOCAL), TB // LOCAL)].reshape(TB, NL)


def turned_tile(buffer, index):
    part = tile(buffer, index)
    return jnp.concatenate([part[:, AVG:], -part[:, :AVG]], axis=1)


def multiply(item, buffers, acc_ref, vis_ref, order_ref, offset, first, last):
    n = order_ref[0, offset + item]
    a = 0
    for k in range(1, INPUTS // TB):
        a = a + (n >= k * (k + 1) // 2).astype(jnp.int32)
    b = n - a * (a + 1) // 2
    straight = jnp.concatenate([tile(buffer, a) for buffer in buffers], axis=1)
    turned = jnp.concatenate([turned_tile(buffer, a) for buffer in buffers], axis=1)
    gram = lax.dot_general(
        jnp.concatenate([straight, turned], axis=0),
        jnp.concatenate([tile(buffer, b) for buffer in buffers], axis=1),
        NT,
        preferred_element_type=jnp.float32,
    )
    if not first:
        gram = gram + acc_ref[item]
    if last:
        vis_ref[0, item] = (gram * MEAN).reshape(2, TB, TB)
    else:
        acc_ref[item] = gram


def make_weights(l, table_ref, index_ref, weight_ref):
    picked = (
        lax.broadcasted_iota(jnp.int32, (NBEAM, NBEAM), 0) == index_ref[...]
    ).astype(jnp.float32).astype(jnp.bfloat16)
    chosen = lax.dot_general(
        picked,
        jnp.concatenate([table_ref[:, 0, :], table_ref[:, 1, :]], axis=1),
        TN,
        preferred_element_type=jnp.float32,
    ).astype(jnp.bfloat16)
    spread = (
        lax.broadcasted_iota(jnp.int32, (STATIONS, INPUTS), 1)
        == 2 * lax.broadcasted_iota(jnp.int32, (STATIONS, INPUTS), 0) + l
    ).astype(jnp.float32).astype(jnp.bfloat16)
    for q in range(2):
        weight_ref[l, pl.ds(q * NBEAM, NBEAM), :] = lax.dot_general(
            chosen[:, q * STATIONS : (q + 1) * STATIONS], spread, NN,
            preferred_element_type=jnp.float32,
        ).astype(jnp.bfloat16)


def form_beams(frames, l, sources, weight_ref, beam_ref):
    spectra = jnp.concatenate([sources[frame][...].reshape(INPUTS, NL) for frame in frames], axis=1)
    sums = lax.dot_general(weight_ref[l], spectra, NN, preferred_element_type=jnp.float32)
    for n, frame in enumerate(frames):
        straight = sums[:NBEAM, n * NL : (n + 1) * NL]
        crossed = sums[NBEAM:, n * NL : (n + 1) * NL]
        crossed = jnp.concatenate([-crossed[:, AVG:], crossed[:, :AVG]], axis=1)
        voltage = straight + crossed
        power = (voltage * voltage).T
        beam_ref[l, frame] = power[:AVG] + power[AVG:]


def correlator_kernel(
    volts_hbm, coefs_hbm, first_hbm, twid_hbm, second_hbm, order_hbm, table_hbm, index_hbm,
    vis_ref, beam_ref,
    volts_ref, coefs_ref, first_ref, twid_ref, second_ref, order_ref, table_ref, index_ref,
    own_ref, spread_ref, past_ref, next_ref, coef_ref, rows_ref, send_ref,
    mine1, mine2, mine3, mine4, left1, left2, left3, left4,
    right1, right2, right3, right4, far1, far2, far3, far4,
    acc_ref, weight_ref,
    load_sem, halo_send, halo_recv, out_sem, in_sem, ysend_sem, yin_sem,
):
    section = lax.axis_index("section")
    chan = lax.axis_index("chan")
    x, z, core = chan // XBLOCK, (chan % XBLOCK) // NCORE, chan % NCORE
    right, left = (section + 1) % NSEC, (section + NSEC - 1) % NSEC
    mine = {1: mine1, 2: mine2, 3: mine3, 4: mine4}
    lefts = {1: left1, 2: left2, 3: left3, 4: left4}
    rights = {1: right1, 2: right2, 3: right3, 4: right4}
    fars = {1: far1, 2: far2, 3: far3, 4: far4}

    arrays = (
        (volts_hbm, volts_ref), (coefs_hbm, coefs_ref), (first_hbm, first_ref),
        (twid_hbm, twid_ref), (second_hbm, second_ref), (order_hbm, order_ref),
        (table_hbm, table_ref), (index_hbm, index_ref),
    )
    loads = [
        pltpu.make_async_copy(source, target, load_sem.at[n])
        for n, (source, target) in enumerate(arrays)
    ]
    for load in loads:
        load.start()

    barrier = pltpu.get_barrier_semaphore()

    @pl.loop(1, NCHAN)
    def _(k):
        pl.semaphore_signal(
            barrier, inc=1, device_id=(section, (chan + k) % NCHAN), device_id_type=MESH
        )

    for other in (left, right):
        pl.semaphore_signal(barrier, inc=1, device_id=(other, chan), device_id_type=MESH)

    def sources(q, i, t):
        if t < 0:
            return past_ref[t + 2, q, i]
        return own_ref[q, i, t] if t < FRAMES else next_ref[q, i]

    def spread_coefficients():
        keep = jnp.where(section < NSEC - 1, 1.0, 0.0)
        for a in range(NA):
            coef_ref[0, pl.ds(a, TAPS, stride=NA), :] = coefs_ref[:, a * NL : (a + 1) * NL]
        coef_ref[1, :NA] = coef_ref[0, :NA]
        coef_ref[1, NA:] = coef_ref[0, NA:] * keep

    def fft(frame):
        transform(
            frame, 0, LOCAL, sources, coef_ref.at[1 if frame == FRAMES else 0],
            first_ref, twid_ref, second_ref, rows_ref,
        )

    def halo(t):
        if t == FRAMES:
            source, target, peer = own_ref.at[:, :, 0], next_ref, left
        else:
            source, target, peer = own_ref.at[:, :, t + FRAMES], past_ref.at[t + 2], right
        return pltpu.make_async_remote_copy(
            src_ref=source,
            dst_ref=target,
            send_sem=halo_send.at[HALOS.index(t)],
            recv_sem=halo_recv.at[HALOS.index(t)],
            device_id=(peer, chan),
            device_id_type=MESH,
        )

    def halo_wait(t):
        halo(t).wait_recv()
        if t < 0:

            @pl.when(section == 0)
            def _():
                past_ref[t + 2] = jnp.zeros(past_ref.shape[1:], jnp.bfloat16)

    def piece(frame, dx, dz, dc):
        peer = (
            lax.rem(x + dx, NX) * XBLOCK + lax.rem(z + dz, NZ) * NCORE + lax.rem(core + dc, NCORE)
        )
        return pltpu.make_async_remote_copy(
            src_ref=send_ref.at[frame - 1, peer],
            dst_ref=mine[frame].at[chan],
            send_sem=out_sem.at[frame - 1, dx],
            recv_sem=in_sem.at[frame - 1, dx],
            device_id=(section, peer),
            device_id_type=MESH,
        )

    def ready(frame):
        send_ref[frame - 1] = rows_ref[...].astype(jnp.bfloat16).reshape(NCHAN, LOCAL, NL)
        pltpu.make_async_copy(
            send_ref.at[frame - 1, chan], mine[frame].at[chan], in_sem.at[frame - 1, 0]
        ).start()

    def scatter(frame, dx):
        for dz in ZORDER:
            for dc in range(NCORE):
                if (dx, dz, dc) != (0, 0, 0):
                    piece(frame, dx, dz, dc).start()

    def ycopy(source, target, dx, peer, frame, slot):
        part = pl.ds(((x + NX - dx) % NX) * XBLOCK, XBLOCK)
        return pltpu.make_async_remote_copy(
            src_ref=source[frame].at[part],
            dst_ref=target[frame].at[part],
            send_sem=ysend_sem.at[frame - 1, dx, slot],
            recv_sem=yin_sem.at[frame - 1, dx, slot],
            device_id=(peer, chan),
            device_id_type=MESH,
        )

    def to_right(frame, dx):
        return ycopy(mine, lefts, dx, right, frame, 0)

    def to_left(frame, dx):
        return ycopy(mine, rights, dx, left, frame, 1)

    def onward(frame, dx):
        if (frame, dx) in BY_RIGHT:
            return ycopy(lefts, fars, dx, right, frame, 2)
        return ycopy(rights, fars, dx, left, frame, 2)

    def forward(frame, dx):
        part = mine[frame].at[pl.ds(((x + NX - dx) % NX) * XBLOCK, XBLOCK)]
        pltpu.make_async_copy(part, part, in_sem.at[frame - 1, dx]).wait()
        to_left(frame, dx).start()
        to_right(frame, dx).start()

    def relay(frame, dx):
        (to_right if (frame, dx) in BY_RIGHT else to_left)(frame, dx).wait_recv()
        onward(frame, dx).start()

    def near_wait(frame):
        for dx in range(NX):
            (to_left if (frame, dx) in BY_RIGHT else to_right)(frame, dx).wait_recv()

    def far_wait(frame):
        for dx in range(NX):
            onward(frame, dx).wait_recv()

    def products(buffers, first=False, last=False):
        for item in range(ITEMS):
            multiply(
                item, buffers, acc_ref, vis_ref, order_ref, section * ITEMS, first, last
            )

    def weights(l):
        make_weights(l, table_ref, index_ref, weight_ref)

    def beams(frames, l):
        form_beams(frames, l, {**mine, 0: left4}, weight_ref, beam_ref)

    loads[0].wait()
    relayout(volts_ref, own_ref, spread_ref)
    pl.semaphore_wait(barrier, NCHAN + 1)
    for t in (-1, FRAMES, -2):
        halo(t).start()
    for load in loads[1:]:
        load.wait()
    spread_coefficients()
    fft(3)
    ready(3)
    scatter(3, 0)
    scatter(3, 1)
    scatter(3, 2)
    scatter(3, 3)
    forward(3, 0)
    forward(3, 1)
    forward(3, 2)
    forward(3, 3)
    halo_wait(-1)
    fft(2)
    ready(2)
    scatter(2, 0)
    scatter(2, 1)
    scatter(2, 2)
    scatter(2, 3)
    relay(3, 0)
    relay(3, 1)
    halo_wait(FRAMES)
    fft(4)
    ready(4)
    scatter(4, 0)
    scatter(4, 1)
    scatter(4, 2)
    scatter(4, 3)
    relay(3, 2)
    forward(2, 0)
    halo_wait(-2)
    fft(1)
    ready(1)
    scatter(1, 0)
    scatter(1, 1)
    scatter(1, 2)
    scatter(1, 3)
    relay(3, 3)
    forward(2, 1)
    forward(2, 2)
    forward(2, 3)
    relay(2, 0)
    forward(4, 0)
    forward(4, 1)
    relay(2, 1)
    forward(4, 2)
    forward(4, 3)
    relay(2, 2)
    weights(0)
    forward(1, 0)
    relay(2, 3)
    weights(1)
    forward(1, 1)
    relay(4, 0)
    forward(1, 2)
    relay(4, 1)
    forward(1, 3)
    near_wait(3)
    products((mine3, left3, right3), first=True)
    relay(4, 2)
    beams((3, 2), 0)
    relay(4, 3)
    beams((3, 2), 1)
    far_wait(3)
    near_wait(2)
    products((far3, mine2, left2, right2))
    relay(1, 0)
    near_wait(4)
    beams((1, 0), 0)
    relay(1, 1)
    beams((1, 0), 1)
    relay(1, 2)
    far_wait(2)
    products((far2, mine4, left4, right4))
    relay(1, 3)
    far_wait(4)
    near_wait(1)
    products((far4, mine1, left1, right1))
    far_wait(1)
    products((far1,), last=True)

    for t in (-1, FRAMES, -2):
        halo(t).wait_send()
    for frame in CHUNKS:
        for dx in range(NX):
            for copy in (to_right, to_left, onward):
                copy(frame, dx).wait_send()
            sent = send_ref.at[frame - 1, pl.ds(0, XBLOCK - 1 if dx == 0 else XBLOCK)]
            pltpu.make_async_copy(sent, sent, out_sem.at[frame - 1, dx]).wait()


def store_kernel(vis_ref, beam_ref, vis_hbm, beam_hbm, sems):
    copies = [
        pltpu.make_async_copy(vis_ref, vis_hbm, sems.at[0]),
        pltpu.make_async_copy(beam_ref, beam_hbm, sems.at[1]),
    ]
    for copy in copies:
        copy.start()
    for copy in copies:
        copy.wait()


def shards(voltages, coefficients, tile_order, steer_table, beam_index):
    vmem = pl.BlockSpec(memory_space=pltpu.VMEM)
    hbm = pl.BlockSpec(memory_space=pltpu.HBM)
    first, twiddle, second = tables()
    visibility, beam_power = pl.pallas_call(
        correlator_kernel,
        out_shape=(
            pltpu.VMEM((1, ITEMS, 2, TB, TB), jnp.float32),
            pltpu.VMEM((2, FRAMES, AVG, NBEAM), jnp.float32),
        ),
        in_specs=[hbm] * 8,
        out_specs=(vmem, vmem),
        scratch_shapes=[
            pltpu.VMEM(voltages.shape, voltages.dtype),
            pltpu.VMEM(coefficients.shape, coefficients.dtype),
            pltpu.VMEM(first.shape, first.dtype),
            pltpu.VMEM(twiddle.shape, twiddle.dtype),
            pltpu.VMEM(second.shape, second.dtype),
            pltpu.SMEM(tile_order.shape, tile_order.dtype),
            pltpu.VMEM(steer_table.shape, steer_table.dtype),
            pltpu.VMEM((1, NBEAM), beam_index.dtype),
            pltpu.VMEM((2, LOCAL, FRAMES, NA, NL), jnp.bfloat16),
            pltpu.VMEM((8, FRAMES * NA, NL), jnp.float32),
            pltpu.VMEM((2, 2, LOCAL, NA, NL), jnp.bfloat16),
            pltpu.VMEM((2, LOCAL, NA, NL), jnp.bfloat16),
            pltpu.VMEM((2, TAPS * NA, NL), jnp.float32),
            pltpu.VMEM((NCHAN * LOCAL, NL), jnp.float32),
            pltpu.VMEM((FRAMES, NCHAN, LOCAL, NL), jnp.bfloat16),
        ]
        + [pltpu.VMEM((NCHAN, LOCAL, NL), jnp.bfloat16)] * (4 * FRAMES)
        + [
            pltpu.VMEM((ITEMS, 2 * TB, TB), jnp.float32),
            pltpu.VMEM((2, 2 * NBEAM, INPUTS), jnp.bfloat16),
            pltpu.SemaphoreType.DMA((8,)),
            pltpu.SemaphoreType.DMA((3,)),
            pltpu.SemaphoreType.DMA((3,)),
            pltpu.SemaphoreType.DMA((FRAMES, NX)),
            pltpu.SemaphoreType.DMA((FRAMES, NX)),
            pltpu.SemaphoreType.DMA((FRAMES, NX, 3)),
            pltpu.SemaphoreType.DMA((FRAMES, NX, 3)),
        ],
        compiler_params=pltpu.CompilerParams(
            collective_id=0, has_side_effects=True
        ),
        name="correlator",
    )(
        voltages,
        coefficients,
        first,
        twiddle,
        second,
        tile_order,
        steer_table,
        beam_index.reshape(1, NBEAM),
    )
    visibility, beam_power = pl.pallas_call(
        store_kernel,
        out_shape=(
            jax.ShapeDtypeStruct(visibility.shape, visibility.dtype),
            jax.ShapeDtypeStruct(beam_power.shape, beam_power.dtype),
        ),
        in_specs=[vmem, vmem],
        out_specs=(hbm, hbm),
        scratch_shapes=[pltpu.SemaphoreType.DMA((2,))],
        compiler_params=pltpu.CompilerParams(vmem_limit_bytes=4 * 1024 * 1024),
        name="store",
    )(visibility, beam_power)
    return visibility, jnp.transpose(beam_power, (0, 3, 1, 2))


def solution(mesh):
    placed = (P(None, "chan", "section", None), P(), P("chan", None), P(), P(None, "chan"))
    return jax.shard_map(
        shards,
        mesh=mesh,
        in_specs=placed,
        out_specs=(P("chan", "section", None, None, None), P(None, None, "section", "chan")),
        check_vma=False,
    )
```
